512 devices in a mesh: slab: 16 (over y, core), tile: 32 (over x, z).
Axes of the slice: x: 4, y: 8, z: 8, core: 2. Of those that a mesh axis runs over, the one named last changes fastest.
Arguments:
- starting_heat_state: float32 [64, 256, 2048], P('slab', 'tile'), may hold values from 0 to 2
- spot_middle_sequence: int32 [2, 2], replicated, may hold values from 0 to 2047, as said below
- crystal_label_field: int32 [128, 64, 4096], P('slab', None, 'tile'), may hold values from 0 to 4095
- growth_front_radius: float32 [128, 64, 4096], P('slab', None, 'tile'), may hold values from 0 to 1
- seed_voxel_position: int32 [32768], P(('slab', 'tile')), may hold values from 0 to 65535, as said below
- seed_crystal_label: int32 [32768], P(('slab', 'tile')), may hold values from 0 to 4095
Outputs:
- heated_state_result: float32 [64, 256, 2048], P('slab', 'tile')
- grown_envelope: float32 [128, 64, 4096], P('slab', None, 'tile')
The draws below stay inside these ranges and needn't reach their ends.
Inputs may be any that keep to these rules, and one draw needn't show every extreme that they name: `spot_middle_sequence`: beam cells lie on the grid: the first entry below 256, the second below 2048; the last step's scan entry is 2047. `seed_voxel_position`: the sites of one device name distinct cells of its block.
All inputs are finite; a program needn't handle non-finite values.
Results may differ from the reference program's by a relative error of at most 0.00002.
Values sent between devices are 32-bit elements; how exact they have to be, the bound alone decides.
A program may use at most 64 MiB of HBM per device.

```python
import jax
import jax.numpy as jnp
from jax import lax

CZ = 4
YS = 64
WX = 32
SITES_DEV = 64
STEPS = 2
BUILD_LEVELS = 64
SIDEWAYS_SITES = 256
PASS_VOXELS = 2048
FINE_DEV = 65536
SITES_ALL = 32768
N_TILE = 32


def draw_spot_middle_sequence(key, part):
    first = jax.random.randint(jax.random.fold_in(key, 11), (STEPS, 1), 0, SIDEWAYS_SITES)
    second = jax.random.randint(jax.random.fold_in(key, 12), (STEPS, 1), 0, PASS_VOXELS)
    last_row = jnp.arange(STEPS, dtype=jnp.int32)[:, None] == STEPS - 1
    second = jnp.where(last_row, PASS_VOXELS - 1, second)
    return jnp.concatenate([first, second], axis=1).astype(jnp.int32)


def draw_seed_voxel_position(key, part):
    owners = SITES_ALL // SITES_DEV
    stride_cells = FINE_DEV // SITES_DEV
    offsets = jax.random.randint(jax.random.fold_in(key, 21), (owners, SITES_DEV), 0, stride_cells)
    last_site = jnp.arange(SITES_DEV, dtype=jnp.int32)[None, :] == SITES_DEV - 1
    offsets = jnp.where(last_site, stride_cells - 1, offsets)
    base = jnp.arange(SITES_DEV, dtype=jnp.int32) * stride_cells
    return (base[None, :] + offsets).reshape(-1).astype(jnp.int32)


def touch_ends(drawn, rng, smallest, top_value):
    longest = drawn.shape.index(max(drawn.shape))
    spots = []
    for shift in (0, 1):
        where = [jax.random.randint(jax.random.fold_in(rng, axis), (), 0, length) for axis, length in enumerate(drawn.shape)]
        where[longest] = (where[longest] + shift) % drawn.shape[longest]
        spots.append(tuple(where))
    return drawn.at[spots[0]].set(smallest).at[spots[1]].set(top_value)


def levels(key, extent, pieces, least, top_value):
    level = 1.0
    for dim, blocks in pieces:
        heights = jax.random.uniform(jax.random.fold_in(jax.random.fold_in(key, 6), dim), (blocks,), jnp.float32, least / len(pieces), top_value / len(pieces))
        level = level * jnp.repeat(jnp.exp(heights), extent[dim] // blocks).reshape((-1,) + (1,) * (len(extent) - 1 - dim))
    return level


def setup_inputs(seed: int = 0) -> dict:
    key_of = jax.random.split(jax.random.key(seed), 7)
    return {
        "starting_heat_state": jnp.clip(2.0 * jax.random.uniform(key_of[0], (BUILD_LEVELS, SIDEWAYS_SITES, PASS_VOXELS), jnp.float32) ** levels(key_of[0], (BUILD_LEVELS, SIDEWAYS_SITES, PASS_VOXELS), ((0, 16), (1, 32)), -0.2, 0.2), 0.0, 2.0),
        "spot_middle_sequence": draw_spot_middle_sequence(jax.random.fold_in(key_of[6], 71), 0),
        "crystal_label_field": touch_ends(jax.random.randint(key_of[2], (2 * BUILD_LEVELS, 2 * WX, 2 * PASS_VOXELS), 0, 4096), jax.random.fold_in(key_of[2], 1), 0, 4095).astype(jnp.int32),
        "growth_front_radius": jnp.clip(1.0 * jax.random.uniform(key_of[3], (2 * BUILD_LEVELS, 2 * WX, 2 * PASS_VOXELS), jnp.float32) ** levels(key_of[3], (2 * BUILD_LEVELS, 2 * WX, 2 * PASS_VOXELS), ((0, 16), (2, 32)), -0.2, 0.2), 0.0, 1.0),
        "seed_voxel_position": draw_seed_voxel_position(jax.random.fold_in(key_of[6], 71), 0),
        "seed_crystal_label": touch_ends(jax.random.randint(key_of[5], (SITES_ALL,), 0, 4096), jax.random.fold_in(key_of[5], 1), 0, 4095).astype(jnp.int32),
    }


heat_rate = 0.1
source_power = 1.5
beam_radius_sq = 36.0
depth_scale = 3.0
liquidus = 1.0
cell_spacing = 0.5
golden_angle = 2.39996323


def conduct(field):
    square = field * field
    return 1.0 + 0.5 * square / (1.0 + square)


def march_forward(bordered_grid, z_first, x_first, beam, total_z, total_x):
    full = jnp.pad(bordered_grid, ((0, 0), (0, 0), (1, 1)))
    kfull = conduct(full)
    centre = full[1:-1, 1:-1, 1:-1]
    kcentre = kfull[1:-1, 1:-1, 1:-1]
    flux = jnp.zeros_like(centre)
    for offset in ((0, 1, 1), (2, 1, 1), (1, 0, 1), (1, 2, 1), (1, 1, 0), (1, 1, 2)):
        neigh = full[offset[0]:offset[0] + centre.shape[0], offset[1]:offset[1] + centre.shape[1], offset[2]:offset[2] + centre.shape[2]]
        kneigh = kfull[offset[0]:offset[0] + centre.shape[0], offset[1]:offset[1] + centre.shape[1], offset[2]:offset[2] + centre.shape[2]]
        flux = flux + 0.5 * (kcentre + kneigh) * (neigh - centre)
    zcoord = z_first + jnp.arange(centre.shape[0], dtype=jnp.int32)
    xcoord = x_first + jnp.arange(centre.shape[1], dtype=jnp.int32)
    ycoord = jnp.arange(centre.shape[2], dtype=jnp.int32)
    depth = (total_z - 1 - zcoord).astype(jnp.float32)
    xdist = (xcoord - beam[0]).astype(jnp.float32)
    ydist = (ycoord - beam[1]).astype(jnp.float32)
    plane = jnp.exp(-(xdist[:, None] * xdist[:, None] + ydist[None, :] * ydist[None, :]) / beam_radius_sq)
    source = source_power * plane[None, :, :] * jnp.exp(-depth / depth_scale)[:, None, None]
    result = centre + heat_rate * flux + source
    inside = ((zcoord >= 0) & (zcoord < total_z))[:, None, None] & ((xcoord >= 0) & (xcoord < total_x))[None, :, None]
    return jnp.where(inside, result, jnp.zeros_like(result))


def refine_axis(bordered_grid, axis):
    count = bordered_grid.shape[axis] - 2
    before = lax.slice_in_dim(bordered_grid, 0, count, axis=axis)
    centre = lax.slice_in_dim(bordered_grid, 1, count + 1, axis=axis)
    after = lax.slice_in_dim(bordered_grid, 2, count + 2, axis=axis)
    lower = 0.25 * before + 0.75 * centre
    upper = 0.75 * centre + 0.25 * after
    stacked = jnp.stack([lower, upper], axis=axis + 1)
    array_extent = list(centre.shape)
    array_extent[axis] = 2 * count
    return stacked.reshape(array_extent)


def extend_along_dimension(field, axis):
    widths = [(0, 0), (0, 0), (0, 0)]
    widths[axis] = (1, 1)
    return jnp.pad(field, widths)


def grow(fine_temp, nucleated, growth_front_radius):
    theta = golden_angle * (nucleated % 64).astype(jnp.float32)
    speed = 1.0 + 0.5 * jnp.cos(4.0 * theta)
    under = jnp.maximum(liquidus - fine_temp, 0.0)
    return growth_front_radius + speed * under * under


def diffuse_outward(bordered_grid):
    centre = bordered_grid[1:-1, 1:-1, 1:-1]
    winning_choice = centre
    for offset in ((0, 1, 1), (2, 1, 1), (1, 0, 1), (1, 2, 1), (1, 1, 0), (1, 1, 2)):
        neigh = bordered_grid[offset[0]:offset[0] + centre.shape[0], offset[1]:offset[1] + centre.shape[1], offset[2]:offset[2] + centre.shape[2]]
        winning_choice = jnp.maximum(winning_choice, neigh - cell_spacing)
    return winning_choice


def reference(starting_heat_state, spot_middle_sequence, crystal_label_field, growth_front_radius, seed_voxel_position, seed_crystal_label):
    heated_state_result = starting_heat_state
    for single_update in range(STEPS):
        bordered_grid = jnp.pad(heated_state_result, ((1, 1), (1, 1), (0, 0)))
        heated_state_result = march_forward(bordered_grid, 0, 0, spot_middle_sequence[single_update], BUILD_LEVELS, SIDEWAYS_SITES)
    window_first = (SIDEWAYS_SITES - WX) // 2
    broadened_grid = extend_along_dimension(heated_state_result, 1)
    window = lax.slice_in_dim(broadened_grid, window_first, window_first + WX + 2, axis=1)
    fine_temp = refine_axis(extend_along_dimension(window, 0), 0)
    fine_temp = refine_axis(fine_temp, 1)
    fine_temp = refine_axis(extend_along_dimension(fine_temp, 2), 2)
    block_z = 2 * CZ
    block_x = 2 * WX
    block_y = 2 * YS
    owner = jnp.arange(SITES_ALL, dtype=jnp.int32) // SITES_DEV
    slab_index = owner // N_TILE
    tile_index = owner % N_TILE
    local_z = seed_voxel_position // (block_x * block_y)
    remain = seed_voxel_position % (block_x * block_y)
    local_x = remain // block_y
    local_y = remain % block_y
    nucleated = crystal_label_field.at[slab_index * block_z + local_z, local_x, tile_index * block_y + local_y].set(seed_crystal_label)
    grown = grow(fine_temp, nucleated, growth_front_radius)
    bordered_grid = jnp.pad(grown, ((1, 1), (1, 1), (1, 1)))
    return heated_state_result, diffuse_outward(bordered_grid)
```

```python
import jax
import jax.numpy as jnp
from jax import lax
from jax.experimental import pallas as pl
from jax.experimental.pallas import tpu as pltpu
from jax.sharding import PartitionSpec as P

HEAT_RATE = 0.1
SOURCE_POWER = 1.5
BEAM_RADIUS_SQ = 36.0
DEPTH_SCALE = 3.0
GOLDEN_ANGLE = 2.39996323
MESH = pl.DeviceIdType.MESH
F32 = jnp.float32
NEIGHBOURS = [(a, b) for a in (-1, 0, 1) for b in (-1, 0, 1) if (a, b) != (0, 0)]


def lanes(rows):
    return lax.broadcasted_iota(jnp.int32, (rows, 128), 1)


def lane_pick(x, index):
    return jnp.take_along_axis(x, index, axis=1)


def conductance(v):
    return 0.5 * HEAT_RATE * 1.5 - (0.25 * HEAT_RATE) / (1.0 + v * v)


def next_along_y(x, last):
    r = pltpu.roll(x, 127, 2)
    up = pltpu.roll(r, 15, 1)
    lane = lax.broadcasted_iota(jnp.int32, x.shape, 2)
    row = lax.broadcasted_iota(jnp.int32, x.shape, 1)
    up = jnp.where(row == 15, last, up)
    return jnp.where(lane == 127, up, r)


def before_along_y(x, first):
    r = pltpu.roll(x, 1, 2)
    down = pltpu.roll(r, 1, 1)
    lane = lax.broadcasted_iota(jnp.int32, x.shape, 2)
    row = lax.broadcasted_iota(jnp.int32, x.shape, 1)
    down = jnp.where(row == 0, first, down)
    return jnp.where(lane == 0, down, r)


def heat_step(src, cond, dst, plane, depth, count_z, count_x, offset_x):
    def conductances(z, c):
        cond[z] = conductance(src[z])
        return c

    lax.fori_loop(0, count_z, conductances, 0)

    def layer(z, c):
        v = src[z + 1]
        p = cond[z + 1]
        flux_x = (p[:-1] + p[1:]) * (v[1:] - v[:-1])
        inner = slice(1, count_x - 1)
        vc, pc = v[inner], p[inner]
        total = flux_x[1:] - flux_x[:-1]
        total += (pc + cond[z, 1 : count_x - 1]) * (src[z, 1 : count_x - 1] - vc)
        total += (pc + cond[z + 2, 1 : count_x - 1]) * (src[z + 2, 1 : count_x - 1] - vc)
        outside = 0.5 * HEAT_RATE
        flux_y = (pc + next_along_y(pc, outside)) * (next_along_y(vc, 0.0) - vc)
        edge = (pc + outside) * vc
        low = jnp.broadcast_to(edge[:, 0:1, 0:1], vc.shape)
        total += flux_y - before_along_y(flux_y, low)
        source = plane[offset_x : offset_x + count_x - 2] * depth[z]
        dst[z] = vc + total + source
        return c

    lax.fori_loop(0, count_z - 2, layer, 0)


def kernel(
    n_slab,
    n_tile,
    x_in,
    spot_in,
    lab_in,
    rad_in,
    pos_in,
    seed_in,
    heat_out,
    grown_out,
    x_v,
    spot,
    lab,
    rad,
    pos,
    seed,
    spd,
    E,
    PE,
    M,
    H,
    plane,
    depth,
    pk,
    hrow,
    ek,
    W,
    Ph,
    Pe,
    X,
    face_rad,
    face_spd,
    cols,
    col_in,
    side_rad,
    side_spd,
    Gf,
    env,
    in_sem,
    out_sem,
    send_a,
    recv_a,
    send_b,
    recv_b,
    ready,
):
    s = lax.axis_index("slab")
    t = lax.axis_index("tile")
    main = tuple(range(n_tile // 2 - 2, n_tile // 2 + 2))
    edges = (main[0] - 1, main[-1] + 1)
    sources = (edges[0],) + main + (edges[1],)
    is_main = (t >= main[0]) & (t <= main[-1])
    is_source = (t >= sources[0]) & (t <= sources[-1])
    is_edge = is_source & jnp.logical_not(is_main)

    def there(a, b):
        c = jnp.bool_(True)
        if a == -1:
            c = c & (s > 0)
        if a == 1:
            c = c & (s < n_slab - 1)
        if b == -1:
            c = c & (t > 0)
        if b == 1:
            c = c & (t < n_tile - 1)
        return c

    bar = pltpu.get_barrier_semaphore()
    count = jnp.int32(0)
    for a, b in NEIGHBOURS:
        c = there(a, b)

        @pl.when(c)
        def _():
            pl.semaphore_signal(bar, inc=1, device_id=(s + a, t + b), device_id_type=MESH)

        count = count + c.astype(jnp.int32)

    @pl.when(is_source)
    def _():
        @pl.loop(0, n_tile)
        def _(d):
            @pl.when(d != t)
            def _():
                pl.semaphore_signal(bar, inc=1, device_id=(s, d), device_id_type=MESH)

    count = count + len(sources) - is_source.astype(jnp.int32)

    loads = [
        pltpu.make_async_copy(a, b, in_sem.at[i])
        for i, (a, b) in enumerate(
            (
                (x_in, x_v),
                (lab_in, lab),
                (rad_in, rad),
                (spot_in, spot),
                (pos_in, pos),
                (seed_in, seed),
            )
        )
    ]
    for c in loads:
        c.start()

    @pl.when(s == 0)
    def _():
        E[0:3] = jnp.zeros((3,) + E.shape[1:], F32)

    @pl.when(s == n_slab - 1)
    def _():
        E[7:10] = jnp.zeros((3,) + E.shape[1:], F32)

    @pl.when(t == 0)
    def _():
        E[:, 0:2] = jnp.zeros((10, 2) + E.shape[2:], F32)
        col_in[0] = jnp.zeros(col_in.shape[1:], F32)

    @pl.when(t == n_tile - 1)
    def _():
        E[:, 10:12] = jnp.zeros((10, 2) + E.shape[2:], F32)
        col_in[1] = jnp.zeros(col_in.shape[1:], F32)

    @pl.when(s == 0)
    def _():
        face_rad[0] = jnp.zeros((64, 128), F32)
        face_spd[0] = jnp.zeros((64, 128), F32)

    @pl.when(s == n_slab - 1)
    def _():
        face_rad[1] = jnp.zeros((64, 128), F32)
        face_spd[1] = jnp.zeros((64, 128), F32)

    loads[0].wait()
    flat = E.reshape(10 * 12 * 16, 128)
    for z in range(4):
        for k in range(16):
            row = ((z + 3) * 12 + 2) * 16 + k
            flat[pl.ds(row, 8, stride=16), :] = x_v[z, :, 128 * k : 128 * k + 128]

    pl.semaphore_wait(bar, count)

    halos = []
    for a, b in NEIGHBOURS:
        zs = {0: (3, 4, 3), -1: (3, 3, 7), 1: (4, 3, 0)}[a]
        xs = {0: (2, 8, 2), -1: (2, 2, 10), 1: (8, 2, 0)}[b]
        if a != 0 and b != 0:
            zs = {-1: (3, 2, 7), 1: (5, 2, 1)}[a]
        k = len(halos)
        halos.append(
            (
                a,
                b,
                pltpu.make_async_remote_copy(
                    src_ref=E.at[pl.ds(zs[0], zs[1]), pl.ds(xs[0], xs[1])],
                    dst_ref=E.at[pl.ds(zs[2], zs[1]), pl.ds(xs[2], xs[1])],
                    send_sem=send_a.at[k],
                    recv_sem=recv_a.at[k],
                    device_id=(s + a, t + b),
                    device_id_type=MESH,
                ),
            )
        )
    for a, b, copy in halos:

        @pl.when(there(a, b))
        def _():
            copy.start()

    for q in sources:

        @pl.when(t != q)
        def _():
            pl.semaphore_signal(ready, inc=1, device_id=(s, jnp.int32(q)), device_id_type=MESH)

    for c in loads[1:]:
        c.wait()
    place = pos[...].reshape(1, 64)
    value = ((seed[...].reshape(1, 64) & 63) + 1).astype(F32)
    rows = lax.broadcasted_iota(jnp.int32, (512, 64), 0)
    cells = lax.broadcasted_iota(jnp.int32, (128, 64), 0)
    in_row = jnp.where(rows == (place >> 7), 1.0, 0.0).astype(jnp.bfloat16)
    in_lane = jnp.where(cells == (place & 127), value, 0.0).astype(jnp.bfloat16)
    named = lax.dot_general(
        in_row, in_lane, (((1,), (1,)), ((), ())), preferred_element_type=F32
    ).reshape(8, 64, 128)
    theta = GOLDEN_ANGLE * lanes(8).astype(F32)
    table = 1.0 + 0.5 * jnp.cos(4.0 * theta)
    table = jnp.broadcast_to(table[0:1], (64, 128))
    for z in range(8):
        grain = jnp.where(named[z] > 0.5, named[z].astype(jnp.int32) - 1, lab[z] & 63)
        spd[z] = lane_pick(table, grain)

    pick_r = lax.broadcasted_iota(jnp.int32, (8, 128), 0)
    lane8 = lanes(8)
    nt = (((1,), (1,)), ((), ()))
    e_rad = jnp.where(
        ((pick_r == 0) & (lane8 == 127)) | ((pick_r == 2) & (lane8 == 0)), 1.0, 0.0
    )
    e_spd = jnp.where(
        ((pick_r == 1) & (lane8 == 127)) | ((pick_r == 3) & (lane8 == 0)), 1.0, 0.0
    )
    hi = lax.Precision.HIGHEST
    cols[...] = lax.dot_general(
        e_rad, rad[...].reshape(512, 128), nt, precision=hi, preferred_element_type=F32
    ) + lax.dot_general(
        e_spd, spd[...].reshape(512, 128), nt, precision=hi, preferred_element_type=F32
    )

    for step in range(2):
        row = lax.broadcasted_iota(jnp.int32, (12, 16, 128), 0)
        y = lax.broadcasted_iota(jnp.int32, (12, 16, 128), 1) * 128
        y = y + lax.broadcasted_iota(jnp.int32, (12, 16, 128), 2)
        xd = (t * 8 - 2 + row - spot[step, 0]).astype(F32)
        yd = (y - spot[step, 1]).astype(F32)
        plane[step] = SOURCE_POWER * jnp.exp(-(xd * xd + yd * yd) / BEAM_RADIUS_SQ)
    level = lax.broadcasted_iota(jnp.int32, (8, 16, 128), 0) + (s * 4 - 2)
    depth[...] = jnp.exp(-(n_slab * 4 - 1 - level).astype(F32) / DEPTH_SCALE)

    fine = []
    k0 = len(NEIGHBOURS)
    for a, z in ((1, 7), (-1, 0)):
        slot = 0 if a == 1 else 1
        fine.append((a, 0, rad.at[z], face_rad.at[slot], (s + a, t)))
        fine.append((a, 0, spd.at[z], face_spd.at[slot], (s + a, t)))
    for b in (1, -1):
        slot = 0 if b == 1 else 1
        fine.append((0, b, cols, col_in.at[slot], (s, t + b)))
    fine = [
        (
            a,
            b,
            pltpu.make_async_remote_copy(
                src_ref=src,
                dst_ref=dst,
                send_sem=send_a.at[k0 + i],
                recv_sem=recv_a.at[k0 + i],
                device_id=to,
                device_id_type=MESH,
            ),
        )
        for i, (a, b, src, dst, to) in enumerate(fine)
    ]
    for a, b, copy in fine:

        @pl.when(there(a, b))
        def _():
            copy.start()

    for a, b, copy in halos:

        @pl.when(there(-a, -b))
        def _():
            copy.wait_recv()

    for a, b, copy in halos:

        @pl.when(there(a, b))
        def _():
            copy.wait_send()

    heat_step(E, PE, M, plane.at[0], depth, 10, 12, 1)

    @pl.when(s == 0)
    def _():
        M[0:2] = jnp.zeros((2,) + M.shape[1:], F32)

    @pl.when(s == n_slab - 1)
    def _():
        M[6:8] = jnp.zeros((2,) + M.shape[1:], F32)

    @pl.when(t == 0)
    def _():
        M[:, 0:1] = jnp.zeros((8, 1) + M.shape[2:], F32)

    @pl.when(t == n_tile - 1)
    def _():
        M[:, 9:10] = jnp.zeros((8, 1) + M.shape[2:], F32)

    heat_step(M, PE.at[0:8, 0:10], H, plane.at[1], depth.at[1:7], 8, 10, 2)

    @pl.when(s == 0)
    def _():
        H[0] = jnp.zeros(H.shape[1:], F32)

    @pl.when(s == n_slab - 1)
    def _():
        H[5] = jnp.zeros(H.shape[1:], F32)

    Hf = H.reshape(6 * 8 * 16, 128)

    def cut(read, n):
        lane = lanes(n)

        def pieces(k):
            now = [read(z, k) for z in range(6)]
            low = [jnp.where(k > 0, read(z, jnp.maximum(k - 1, 0)), 0.0) for z in range(6)]
            top = [jnp.where(k < 15, read(z, jnp.minimum(k + 1, 15)), 0.0) for z in range(6)]
            even, odd = [], []
            for j in range(3):
                even.append(jnp.where(lane < 64, now[j], pltpu.roll(now[j + 3], 64, 1)))
                odd.append(jnp.where(lane < 64, pltpu.roll(now[j], 64, 1), now[j + 3]))
            h_even = jnp.zeros((n, 128), F32)
            h_odd = jnp.zeros((n, 128), F32)
            for z in range(6):
                here = pltpu.roll(now[z], 65 + 2 * z, 1)
                h_even = jnp.where(lane == 2 * z, pltpu.roll(low[z], 1 + 2 * z, 1), h_even)
                h_even = jnp.where(lane == 2 * z + 1, here, h_even)
                h_odd = jnp.where(lane == 2 * z, here, h_odd)
                h_odd = jnp.where(lane == 2 * z + 1, pltpu.roll(top[z], 1 + 2 * z, 1), h_odd)
            return (even, h_even), (odd, h_odd)

        return pieces

    @pl.when(is_main)
    def _():
        get = cut(lambda z, k: Hf[pl.ds(z * 128 + k, 8, stride=16), :], 8)

        @pl.loop(0, 16)
        def _(k):
            for parity, (body, halo) in enumerate(get(k)):
                d = 2 * k + parity
                for j in range(3):
                    pk[d, j] = body[j]
                spread = pltpu.roll(halo, 0, 1, stride=16, stride_axis=0)
                hrow[d] = jnp.sum(spread, axis=0, keepdims=True)

    @pl.when(is_edge)
    def _():
        x_row = jnp.where(t == edges[0], 7, 0)
        get = cut(lambda z, k: Hf[pl.ds(z * 128 + x_row * 16 + k, 1), :], 1)

        @pl.loop(0, 16)
        def _(k):
            for parity, (body, halo) in enumerate(get(k)):
                d = 2 * k + parity
                for j in range(3):
                    ek[d, j] = body[j]
                ek[d, 3] = halo

    @pl.when(is_source)
    def _():
        pl.semaphore_wait(ready, n_tile - 1)

    def to_slab(d, i):
        own = jnp.int32(i) if isinstance(i, int) else i
        at = pl.multiple_of(own * 8 + 8, 8)
        return (
            pltpu.make_async_remote_copy(
                src_ref=pk.at[d],
                dst_ref=W.at[pl.ds(0, 3), pl.ds(at, 8)],
                send_sem=send_b.at[0],
                recv_sem=recv_b.at[0, own],
                device_id=(s, d),
                device_id_type=MESH,
            ),
            pltpu.make_async_remote_copy(
                src_ref=hrow.at[d],
                dst_ref=Ph.at[own],
                send_sem=send_b.at[1],
                recv_sem=recv_b.at[1, own],
                device_id=(s, d),
                device_id_type=MESH,
            ),
        )

    def edge_to_slab(d, i):
        own = jnp.int32(i) if isinstance(i, int) else i
        return pltpu.make_async_remote_copy(
            src_ref=ek.at[d],
            dst_ref=Pe.at[own],
            send_sem=send_b.at[0],
            recv_sem=recv_b.at[2, own],
            device_id=(s, d),
            device_id_type=MESH,
        )

    @pl.when(is_main)
    def _():
        own = t - main[0]

        @pl.loop(0, n_tile)
        def _(d):
            @pl.when(d != t)
            def _():
                for copy in to_slab(d, own):
                    copy.start()

        at = pl.multiple_of(own * 8 + 8, 8)
        W[0:3, pl.ds(at, 8), :] = pk[t]
        Ph[own] = hrow[t]

    @pl.when(is_edge)
    def _():
        own = jnp.where(t == edges[0], 0, 1)

        @pl.loop(0, n_tile)
        def _(d):
            @pl.when(d != t)
            def _():
                edge_to_slab(d, own).start()

        Pe[own] = ek[t]

    for z in range(4):
        for k in range(16):
            x_v[z, :, 128 * k : 128 * k + 128] = Hf[pl.ds((z + 1) * 128 + k, 8, stride=16), :]
    heat_copy = pltpu.make_async_copy(x_v, heat_out, out_sem.at[0])
    heat_copy.start()

    for a, b, copy in fine:

        @pl.when(there(-a, -b))
        def _():
            copy.wait_recv()

    for a, b, copy in fine:

        @pl.when(there(a, b))
        def _():
            copy.wait_send()

    r16 = lax.broadcasted_iota(jnp.int32, (16, 128), 0)
    l16 = lanes(16)
    both = col_in[...].reshape(16, 512)
    tn = (((0,), (0,)), ((), ()))
    s_rad = jnp.where(((r16 == 0) & (l16 == 0)) | ((r16 == 10) & (l16 == 127)), 1.0, 0.0)
    s_spd = jnp.where(((r16 == 1) & (l16 == 0)) | ((r16 == 11) & (l16 == 127)), 1.0, 0.0)
    side_rad[...] = lax.dot_general(
        both, s_rad, tn, precision=hi, preferred_element_type=F32
    ).reshape(8, 64, 128)
    side_spd[...] = lax.dot_general(
        both, s_spd, tn, precision=hi, preferred_element_type=F32
    ).reshape(8, 64, 128)
    for z in range(10):
        Gf[z, 0:8] = jnp.zeros((8, 128), F32)
        Gf[z, 72:80] = jnp.zeros((8, 128), F32)

    for i, q in enumerate(main):

        @pl.when(t != q)
        def _():
            for copy in to_slab(t, i):
                copy.wait_recv()

    for i, q in enumerate(edges):

        @pl.when(t != q)
        def _():
            edge_to_slab(t, i).wait_recv()

    spot_of = (lane8 + 16 * pick_r) & 127
    for i in range(4):
        W[3, 8 + 8 * i : 16 + 8 * i] = lane_pick(jnp.broadcast_to(Ph[i], (8, 128)), spot_of)
    for j in range(4):
        W[j, 7:8] = Pe[0, j]
        W[j, 40:41] = Pe[1, j]

    Xf = X.reshape(4 * 64, 128)
    for j in range(4):
        low, mid, top = W[j, 7:39], 0.75 * W[j, 8:40], W[j, 9:41]
        Xf[pl.ds(64 * j, 32, stride=2), :] = 0.25 * low + mid
        Xf[pl.ds(64 * j + 1, 32, stride=2), :] = mid + 0.25 * top

    lane = lanes(64)
    half = lane >> 1
    near = jnp.clip(half + jnp.where((lane & 1) == 1, 1, -1), 0, 63)
    rim = (lane == 0) | (lane == 127)
    fine_y, side_y = [], []
    for z in range(6):
        base = 0 if z < 3 else 64
        x = X[z % 3]
        u = lane_pick(x, half + base)
        h = lane_pick(X[3], jnp.where(lane == 127, 2 * z + 1, 2 * z))
        v = jnp.where(rim, h, lane_pick(x, near + base))
        fine_y.append(0.75 * u + 0.25 * v)
        side_y.append(0.75 * h + 0.25 * u)

    def at_height(f, zf):
        z = zf // 2
        if zf % 2 == 0:
            return 0.25 * f[z] + 0.75 * f[z + 1]
        return 0.75 * f[z + 1] + 0.25 * f[z + 2]

    def grow(temp, speed, radius):
        under = jnp.maximum(1.0 - temp, 0.0)
        return radius + speed * under * under

    for zf in range(-1, 9):
        if zf == -1:
            sp, ra = face_spd[0], face_rad[0]
        elif zf == 8:
            sp, ra = face_spd[1], face_rad[1]
        else:
            sp, ra = spd[zf], rad[zf]
        Gf[zf + 1, 8:72] = grow(at_height(fine_y, zf), sp, ra)
    for zf in range(8):
        side = grow(at_height(side_y, zf), side_spd[zf], side_rad[zf])
        c = Gf[zf + 1, 8:72]
        near_y = jnp.maximum(
            jnp.where(lane == 0, side, pltpu.roll(c, 1, 1)),
            jnp.where(lane == 127, side, pltpu.roll(c, 127, 1)),
        )
        near_x = jnp.maximum(Gf[zf + 1, 7:71], Gf[zf + 1, 9:73])
        near_z = jnp.maximum(Gf[zf, 8:72], Gf[zf + 2, 8:72])
        env[zf] = jnp.maximum(c, jnp.maximum(jnp.maximum(near_x, near_y), near_z) - 0.5)
    env_copy = pltpu.make_async_copy(env, grown_out, out_sem.at[1])
    env_copy.start()

    @pl.when(is_main)
    def _():
        @pl.loop(0, n_tile - 1)
        def _(d):
            for copy in to_slab(d, 0):
                copy.wait_send()

    @pl.when(is_edge)
    def _():
        @pl.loop(0, n_tile - 1)
        def _(d):
            edge_to_slab(d, 0).wait_send()

    heat_copy.wait()
    env_copy.wait()


def local(temperature, spot, labels, radius, position, seeds):
    n_slab, n_tile = lax.axis_size("slab"), lax.axis_size("tile")
    any_spec = pl.BlockSpec(memory_space=pl.ANY)
    vm = pltpu.VMEM
    dma = pltpu.SemaphoreType.DMA
    body = lambda *refs: kernel(n_slab, n_tile, *refs)
    return pl.pallas_call(
        body,
        out_shape=(
            jax.ShapeDtypeStruct((4, 8, 2048), F32),
            jax.ShapeDtypeStruct((8, 64, 128), F32),
        ),
        in_specs=[any_spec] * 6,
        out_specs=(any_spec, any_spec),
        scratch_shapes=[
            vm((4, 8, 2048), F32),
            pltpu.SMEM((2, 2), jnp.int32),
            vm((8, 64, 128), jnp.int32),
            vm((8, 64, 128), F32),
            vm((64,), jnp.int32),
            vm((64,), jnp.int32),
            vm((8, 64, 128), F32),
            vm((10, 12, 16, 128), F32),
            vm((10, 12, 16, 128), F32),
            vm((8, 10, 16, 128), F32),
            vm((6, 8, 16, 128), F32),
            vm((2, 12, 16, 128), F32),
            vm((8, 16, 128), F32),
            vm((32, 3, 8, 128), F32),
            vm((32, 1, 128), F32),
            vm((32, 4, 1, 128), F32),
            vm((4, 48, 128), F32),
            vm((4, 1, 128), F32),
            vm((2, 4, 1, 128), F32),
            vm((4, 64, 128), F32),
            vm((2, 64, 128), F32),
            vm((2, 64, 128), F32),
            vm((8, 512), F32),
            vm((2, 8, 512), F32),
            vm((8, 64, 128), F32),
            vm((8, 64, 128), F32),
            vm((10, 80, 128), F32),
            vm((8, 64, 128), F32),
            dma((6,)),
            dma((2,)),
            dma((14,)),
            dma((14,)),
            dma((2,)),
            dma((3, 4)),
            pltpu.SemaphoreType.REGULAR,
        ],
        compiler_params=pltpu.CompilerParams(collective_id=0, has_side_effects=True),
        name="build_step",
    )(temperature, spot, labels, radius, position, seeds)


def solution(mesh):
    return jax.shard_map(
        local,
        mesh=mesh,
        in_specs=(
            P("slab", "tile", None),
            P(),
            P("slab", None, "tile"),
            P("slab", None, "tile"),
            P(("slab", "tile")),
            P(("slab", "tile")),
        ),
        out_specs=(P("slab", "tile", None), P("slab", None, "tile")),
        check_vma=False,
    )
```

```python
import jax
import jax.numpy as jnp
from jax import lax
from jax.experimental import pallas as pl
from jax.experimental.pallas import tpu as pltpu
from jax.sharding import PartitionSpec as P

HEAT_RATE = 0.1
SOURCE_POWER = 1.5
BEAM_RADIUS_SQ = 36.0
DEPTH_SCALE = 3.0
GOLDEN_ANGLE = 2.39996323
MESH = pl.DeviceIdType.MESH
NZ = 8
F32 = jnp.float32
NEIGHBOURS = [(a, b) for a in (-1, 0, 1) for b in (-1, 0, 1) if (a, b) != (0, 0)]


def lanes(rows):
    return lax.broadcasted_iota(jnp.int32, (rows, 128), 1)


def lane_pick(x, index):
    return jnp.take_along_axis(x, index, axis=1)


def conductance(v):
    return 0.5 * HEAT_RATE * 1.5 - (0.25 * HEAT_RATE) / (1.0 + v * v)


def next_along_y(x, last):
    r = pltpu.roll(x, 127, 2)
    up = pltpu.roll(r, 15, 1)
    lane = lax.broadcasted_iota(jnp.int32, x.shape, 2)
    row = lax.broadcasted_iota(jnp.int32, x.shape, 1)
    up = jnp.where(row == 15, last, up)
    return jnp.where(lane == 127, up, r)


def before_along_y(x, first):
    r = pltpu.roll(x, 1, 2)
    down = pltpu.roll(r, 1, 1)
    lane = lax.broadcasted_iota(jnp.int32, x.shape, 2)
    row = lax.broadcasted_iota(jnp.int32, x.shape, 1)
    down = jnp.where(row == 0, first, down)
    return jnp.where(lane == 0, down, r)


def heat_step(src, cond, dst, plane, depth, count_z, count_x, offset_x):
    def conductances(z, c):
        cond[z] = conductance(src[z])
        return c

    lax.fori_loop(0, count_z, conductances, 0)

    def layer(z, c):
        v = src[z + 1]
        p = cond[z + 1]
        flux_x = (p[:-1] + p[1:]) * (v[1:] - v[:-1])
        inner = slice(1, count_x - 1)
        vc, pc = v[inner], p[inner]
        total = flux_x[1:] - flux_x[:-1]
        total += (pc + cond[z, 1 : count_x - 1]) * (src[z, 1 : count_x - 1] - vc)
        total += (pc + cond[z + 2, 1 : count_x - 1]) * (src[z + 2, 1 : count_x - 1] - vc)
        outside = 0.5 * HEAT_RATE
        flux_y = (pc + next_along_y(pc, outside)) * (next_along_y(vc, 0.0) - vc)
        edge = (pc + outside) * vc
        low = jnp.broadcast_to(edge[:, 0:1, 0:1], vc.shape)
        total += flux_y - before_along_y(flux_y, low)
        source = plane[offset_x : offset_x + count_x - 2] * depth[z]
        dst[z] = vc + total + source
        return c

    lax.fori_loop(0, count_z - 2, layer, 0)


def window_step(src, cond, dst, plane, depth, count_z, keep):
    for z in range(count_z):
        cond[z] = conductance(src[z])
    for z in range(count_z - 2):
        v, p = src[z + 1, 8:56], cond[z + 1, 8:56]
        total = (p + cond[z, 8:56]) * (src[z, 8:56] - v)
        total += (p + cond[z + 2, 8:56]) * (src[z + 2, 8:56] - v)
        total += (p + cond[z + 1, 7:55]) * (src[z + 1, 7:55] - v)
        total += (p + cond[z + 1, 9:57]) * (src[z + 1, 9:57] - v)
        total += (p + pltpu.roll(p, 1, 1)) * (pltpu.roll(v, 1, 1) - v)
        total += (p + pltpu.roll(p, 127, 1)) * (pltpu.roll(v, 127, 1) - v)
        at = jnp.broadcast_to(depth[z, 0:1, :], v.shape)
        dst[z, 8:56] = jnp.where(keep, v + total + plane * at, 0.0)


def kernel(
    n_slab,
    n_tile,
    x_in,
    spot_in,
    lab_in,
    rad_in,
    pos_in,
    seed_in,
    heat_out,
    grown_out,
    x_v,
    spot,
    lab,
    rad,
    pos,
    seed,
    spd,
    E,
    PE,
    M,
    H,
    plane,
    depth,
    pk_own,
    pk_out,
    in_own,
    in_out,
    in_sib,
    rl_own,
    rl_out,
    V,
    PV,
    VM,
    VH,
    X,
    face_rad,
    face_spd,
    cols,
    col_in,
    side_rad,
    side_spd,
    Gf,
    env,
    in_sem,
    out_sem,
    send_a,
    recv_a,
    send_b,
    recv_b,
    recv_r,
    send_r,
):
    s = lax.axis_index("slab")
    t = lax.axis_index("tile")
    first = n_tile // 2 - 3
    sources = tuple(range(first, first + 6))
    is_source = (t >= first) & (t < first + 6)
    n_col = n_tile // NZ
    col, pos_z = t // NZ, t % NZ
    odd = s % 2 == 1
    sib = jnp.where(odd, s - 1, s + 1)
    outer = jnp.where(odd, s + 1, s - 1)
    has_outer = (outer >= 0) & (outer < n_slab)

    def sender_of(q):
        return jnp.where((col - q // NZ) % 2 == 0, q, col * NZ + q % NZ)

    relayed = jnp.int32(0)
    is_relay = jnp.bool_(False)
    for i, q in enumerate(sources):
        mine = (pos_z == q % NZ) & ((col - q // NZ) % 2 != 0)
        relayed = jnp.where(mine, i, relayed)
        is_relay = is_relay | mine

    def there(a, b):
        c = jnp.bool_(True)
        if a == -1:
            c = c & (s > 0)
        if a == 1:
            c = c & (s < n_slab - 1)
        if b == -1:
            c = c & (t > 0)
        if b == 1:
            c = c & (t < n_tile - 1)
        return c

    loads = [
        pltpu.make_async_copy(a, b, in_sem.at[i])
        for i, (a, b) in enumerate(
            (
                (x_in, x_v),
                (lab_in, lab),
                (rad_in, rad),
                (spot_in, spot),
                (pos_in, pos),
                (seed_in, seed),
            )
        )
    ]
    for c in loads:
        c.start()

    bar = pltpu.get_barrier_semaphore()
    count = jnp.int32(0)
    for a, b in NEIGHBOURS:
        c = there(a, b)

        @pl.when(c)
        def _():
            pl.semaphore_signal(bar, inc=1, device_id=(s + a, t + b), device_id_type=MESH)

        count = count + c.astype(jnp.int32)
    for q in sources:
        sender = sender_of(q)

        @pl.when(sender != t)
        def _():
            pl.semaphore_signal(bar, inc=1, device_id=(s, sender), device_id_type=MESH)

        @pl.when(has_outer)
        def _():
            pl.semaphore_signal(bar, inc=1, device_id=(outer, sender), device_id_type=MESH)

    @pl.when(is_relay)
    def _():
        pl.semaphore_signal(bar, inc=1, device_id=(s, first + relayed), device_id_type=MESH)

    half_tiles = n_tile // 2
    count = count + jnp.where(
        is_source, half_tiles - 1 + n_col // 2 + jnp.where(has_outer, half_tiles, 0), 0
    )
    count = count + jnp.where(is_relay, NZ - 1 + jnp.where(has_outer, NZ, 0), 0)

    @pl.when(s == 0)
    def _():
        E[0:2] = jnp.zeros((2,) + E.shape[1:], F32)
        V[0:3] = jnp.zeros((3,) + V.shape[1:], F32)
        face_rad[0] = jnp.zeros((64, 128), F32)
        face_spd[0] = jnp.zeros((64, 128), F32)

    @pl.when(s == n_slab - 1)
    def _():
        E[6:8] = jnp.zeros((2,) + E.shape[1:], F32)
        V[7:10] = jnp.zeros((3,) + V.shape[1:], F32)
        face_rad[1] = jnp.zeros((64, 128), F32)
        face_spd[1] = jnp.zeros((64, 128), F32)

    @pl.when(t == 0)
    def _():
        E[:, 0:2] = jnp.zeros((8, 2) + E.shape[2:], F32)
        col_in[0] = jnp.zeros(col_in.shape[1:], F32)

    @pl.when(t == n_tile - 1)
    def _():
        E[:, 10:12] = jnp.zeros((8, 2) + E.shape[2:], F32)
        col_in[1] = jnp.zeros(col_in.shape[1:], F32)

    loads[0].wait()
    flat = E.reshape(8 * 12 * 16, 128)
    for z in range(4):
        for k in range(16):
            row = ((z + 2) * 12 + 2) * 16 + k
            flat[pl.ds(row, 8, stride=16), :] = x_v[z, :, 128 * k : 128 * k + 128]

    lane8 = lanes(8)
    left = lane8 < 64

    @pl.when(is_source)
    def _():
        def read(z, k):
            if k < 0 or k > 15:
                return jnp.zeros((8, 128), F32)
            return x_v[z, :, 128 * k : 128 * k + 128]

        for k in range(16):
            now = [read(z, k) for z in range(4)]
            turned = [pltpu.roll(v, 64, 1) for v in now]
            h_even = jnp.zeros((8, 128), F32)
            h_odd = jnp.zeros((8, 128), F32)
            for z in range(4):
                low, top = read(z, k - 1), read(z, k + 1)
                here = pltpu.roll(now[z], 67 + 6 * z, 1)
                low = pltpu.roll(low, 3 + 6 * z, 1)
                top = pltpu.roll(top, 3 + 6 * z, 1)
                one = (lane8 >= 6 * z) & (lane8 < 6 * z + 3)
                two = (lane8 >= 6 * z + 3) & (lane8 < 6 * z + 6)
                h_even = jnp.where(one, low, jnp.where(two, here, h_even))
                h_odd = jnp.where(one, here, jnp.where(two, top, h_odd))
            for parity, lo, up, halo in ((0, now, turned, h_even), (1, turned, now, h_odd)):
                d = 2 * k + parity
                far = pltpu.roll(halo, 64, 1)
                pk_own[d, 0] = jnp.where(left, lo[0], up[2])
                pk_own[d, 1] = jnp.where(left, lo[1], up[3])
                pk_own[d, 2] = halo
                pk_out[d, 0] = jnp.where(
                    left, jnp.where(odd, lo[1], lo[0]), jnp.where(odd, up[2], up[1])
                )
                pk_out[d, 1] = jnp.where(left, jnp.where(odd, lo[3], lo[2]), far)

    pl.semaphore_wait(bar, count)

    halos = []
    for a, b in NEIGHBOURS:
        zs = {0: (2, 4, 2), -1: (2, 2, 6), 1: (4, 2, 0)}[a]
        xs = {0: (2, 8, 2), -1: (2, 2, 10), 1: (8, 2, 0)}[b]
        if a != 0 and b != 0:
            zs = {-1: (2, 1, 6), 1: (5, 1, 1)}[a]
            xs = {-1: (2, 1, 10), 1: (9, 1, 1)}[b]
        k = len(halos)
        halos.append(
            (
                a,
                b,
                pltpu.make_async_remote_copy(
                    src_ref=E.at[pl.ds(zs[0], zs[1]), pl.ds(xs[0], xs[1])],
                    dst_ref=E.at[pl.ds(zs[2], zs[1]), pl.ds(xs[2], xs[1])],
                    send_sem=send_a.at[k],
                    recv_sem=recv_a.at[k],
                    device_id=(s + a, t + b),
                    device_id_type=MESH,
                ),
            )
        )
    for a, b, copy in sorted(halos, key=lambda h: -h[1]):

        @pl.when(there(a, b))
        def _():
            copy.start()

    def send(kind, src, d, i):
        own = jnp.int32(i) if isinstance(i, int) else i
        return pltpu.make_async_remote_copy(
            src_ref=src,
            dst_ref=(in_own, in_out)[kind].at[own],
            send_sem=send_b.at[kind],
            recv_sem=recv_b.at[kind, own],
            device_id=((s, outer)[kind], d),
            device_id_type=MESH,
        )

    def to_relay(kind, d, at, z):
        return pltpu.make_async_remote_copy(
            src_ref=(pk_own, pk_out)[kind].at[d],
            dst_ref=(rl_own, rl_out)[kind].at[z],
            send_sem=send_b.at[kind],
            recv_sem=recv_r.at[kind, z],
            device_id=(s, at),
            device_id_type=MESH,
        )

    def to_sibling(i):
        return pltpu.make_async_remote_copy(
            src_ref=in_own.at[i],
            dst_ref=in_sib.at[i],
            send_sem=send_r.at[0],
            recv_sem=recv_b.at[2, i],
            device_id=(sib, t),
            device_id_type=MESH,
        )

    @pl.when(is_source)
    def _():
        own = t - first

        @pl.loop(0, NZ)
        def _(z):
            for c in range(0, n_col, 2):
                d = (col + c + 1) % n_col * NZ + z
                at = (col + c + 1) % n_col * NZ + pos_z
                to_relay(0, d, at, z).start()

                @pl.when(has_outer)
                def _():
                    to_relay(1, d, at, z).start()

            for c in range(0, n_col, 2):
                d = (col + c) % n_col * NZ + z

                @pl.when(d != t)
                def _():
                    send(0, pk_own.at[d], d, own).start()

                @pl.when(has_outer)
                def _():
                    send(1, pk_out.at[d], d, own).start()

        in_own[own] = pk_own[t]

    for c in loads[1:]:
        c.wait()
    place = pos[...].reshape(1, 64)
    value = ((seed[...].reshape(1, 64) & 63) + 1).astype(F32)
    rows = lax.broadcasted_iota(jnp.int32, (512, 64), 0)
    cells = lax.broadcasted_iota(jnp.int32, (128, 64), 0)
    in_row = jnp.where(rows == (place >> 7), 1.0, 0.0).astype(jnp.bfloat16)
    in_lane = jnp.where(cells == (place & 127), value, 0.0).astype(jnp.bfloat16)
    named = lax.dot_general(
        in_row, in_lane, (((1,), (1,)), ((), ())), preferred_element_type=F32
    ).reshape(8, 64, 128)
    theta = GOLDEN_ANGLE * lanes(8).astype(F32)
    table = 1.0 + 0.5 * jnp.cos(4.0 * theta)
    table = jnp.broadcast_to(table[0:1], (64, 128))
    for z in range(8):
        grain = jnp.where(named[z] > 0.5, named[z].astype(jnp.int32) - 1, lab[z] & 63)
        spd[z] = lane_pick(table, grain)

    pick_r = lax.broadcasted_iota(jnp.int32, (8, 128), 0)
    nt = (((1,), (1,)), ((), ()))
    e_rad = jnp.where(
        ((pick_r == 0) & (lane8 == 127)) | ((pick_r == 2) & (lane8 == 0)), 1.0, 0.0
    )
    e_spd = jnp.where(
        ((pick_r == 1) & (lane8 == 127)) | ((pick_r == 3) & (lane8 == 0)), 1.0, 0.0
    )
    hi = lax.Precision.HIGHEST
    cols[...] = lax.dot_general(
        e_rad, rad[...].reshape(512, 128), nt, precision=hi, preferred_element_type=F32
    ) + lax.dot_general(
        e_spd, spd[...].reshape(512, 128), nt, precision=hi, preferred_element_type=F32
    )

    sides = []
    lane48 = lanes(48)
    wy = t * 64 + lane48 - jnp.where(lane48 < 100, 0, 128)
    wx = lax.broadcasted_iota(jnp.int32, (48, 128), 0) + first * 8
    for step in range(2):
        row = lax.broadcasted_iota(jnp.int32, (12, 16, 128), 0)
        y = lax.broadcasted_iota(jnp.int32, (12, 16, 128), 1) * 128
        y = y + lax.broadcasted_iota(jnp.int32, (12, 16, 128), 2)
        xd = (t * 8 - 2 + row - spot[step, 0]).astype(F32)
        yd = (y - spot[step, 1]).astype(F32)
        plane[step] = SOURCE_POWER * jnp.exp(-(xd * xd + yd * yd) / BEAM_RADIUS_SQ)
        xd = (wx - spot[step, 0]).astype(F32)
        yd = (wy - spot[step, 1]).astype(F32)
        sides.append(SOURCE_POWER * jnp.exp(-(xd * xd + yd * yd) / BEAM_RADIUS_SQ))
    level = lax.broadcasted_iota(jnp.int32, (8, 16, 128), 0) + (s * 4 - 2)
    depth[...] = jnp.exp(-(n_slab * 4 - 1 - level).astype(F32) / DEPTH_SCALE)

    fine = []
    k0 = len(NEIGHBOURS)
    for a, z in ((1, 7), (-1, 0)):
        slot = 0 if a == 1 else 1
        fine.append((a, 0, rad.at[z], face_rad.at[slot], (s + a, t)))
        fine.append((a, 0, spd.at[z], face_spd.at[slot], (s + a, t)))
    for b in (1, -1):
        slot = 0 if b == 1 else 1
        fine.append((0, b, cols, col_in.at[slot], (s, t + b)))
    fine = [
        (
            a,
            b,
            pltpu.make_async_remote_copy(
                src_ref=src,
                dst_ref=dst,
                send_sem=send_a.at[k0 + i],
                recv_sem=recv_a.at[k0 + i],
                device_id=to,
                device_id_type=MESH,
            ),
        )
        for i, (a, b, src, dst, to) in enumerate(fine)
    ]
    for a, b, copy in fine:

        @pl.when(there(a, b))
        def _():
            copy.start()

    @pl.when(is_relay)
    def _():
        @pl.loop(0, NZ)
        def _(z):
            d = col * NZ + z
            to_relay(0, d, t, z).wait_recv()

            @pl.when(d != t)
            def _():
                send(0, rl_own.at[z], d, relayed).start()

            @pl.when(d == t)
            def _():
                in_own[relayed] = rl_own[z]

            @pl.when(has_outer)
            def _():
                to_relay(1, d, t, z).wait_recv()
                send(1, rl_out.at[z], d, relayed).start()

    for a, b, copy in halos:

        @pl.when(there(-a, -b))
        def _():
            copy.wait_recv()

    for a, b, copy in halos:

        @pl.when(there(a, b))
        def _():
            copy.wait_send()

    heat_step(E, PE, M, plane.at[0], depth.at[1:7], 8, 12, 1)

    @pl.when(s == 0)
    def _():
        M[0:1] = jnp.zeros((1,) + M.shape[1:], F32)

    @pl.when(s == n_slab - 1)
    def _():
        M[5:6] = jnp.zeros((1,) + M.shape[1:], F32)

    @pl.when(t == 0)
    def _():
        M[:, 0:1] = jnp.zeros((6, 1) + M.shape[2:], F32)

    @pl.when(t == n_tile - 1)
    def _():
        M[:, 9:10] = jnp.zeros((6, 1) + M.shape[2:], F32)

    heat_step(M, PE.at[0:6, 0:10], H, plane.at[1], depth.at[2:6], 6, 10, 2)

    Hf = H.reshape(4 * 8 * 16, 128)
    for z in range(4):
        for k in range(16):
            x_v[z, :, 128 * k : 128 * k + 128] = Hf[pl.ds(z * 128 + k, 8, stride=16), :]
    heat_copy = pltpu.make_async_copy(x_v, heat_out, out_sem.at[0])
    heat_copy.start()

    for a, b, copy in fine:

        @pl.when(there(-a, -b))
        def _():
            copy.wait_recv()

    for a, b, copy in fine:

        @pl.when(there(a, b))
        def _():
            copy.wait_send()

    r16 = lax.broadcasted_iota(jnp.int32, (16, 128), 0)
    l16 = lanes(16)
    both = col_in[...].reshape(16, 512)
    tn = (((0,), (0,)), ((), ()))
    s_rad = jnp.where(((r16 == 0) & (l16 == 0)) | ((r16 == 10) & (l16 == 127)), 1.0, 0.0)
    s_spd = jnp.where(((r16 == 1) & (l16 == 0)) | ((r16 == 11) & (l16 == 127)), 1.0, 0.0)
    side_rad[...] = lax.dot_general(
        both, s_rad, tn, precision=hi, preferred_element_type=F32
    ).reshape(8, 64, 128)
    side_spd[...] = lax.dot_general(
        both, s_spd, tn, precision=hi, preferred_element_type=F32
    ).reshape(8, 64, 128)
    for z in range(10):
        Gf[z, 0:8] = jnp.zeros((8, 128), F32)
        Gf[z, 72:80] = jnp.zeros((8, 128), F32)

    for i, q in enumerate(sources):

        @pl.when(sender_of(q) != t)
        def _():
            send(0, pk_own.at[0], t, i).wait_recv()

        to_sibling(i).start()

        @pl.when(has_outer)
        def _():
            send(1, pk_out.at[0], t, i).wait_recv()

    far_lane = jnp.where(lane8 >= 100, lane8 - 125, lane8 - 61)

    def put(i, z, tile, high, halo, base):
        body = pltpu.roll(tile, 64, 1) if high else tile
        around = lane_pick(halo, (far_lane + base) & 127)
        V[z, 8 + 8 * i : 16 + 8 * i] = jnp.where(left, body, around)

    for i in range(6):
        for z in range(4):
            put(i, 3 + z, in_own[i, z % 2], z >= 2, in_own[i, 2], 6 * z)

    @pl.when(has_outer)
    def _():
        at = jnp.where(odd, 7, 0)
        base = 64 + jnp.where(odd, 0, 6)
        for i in range(6):
            for z in range(3):
                put(i, at + z, in_out[i, z // 2], z == 1, in_out[i, 1], base + 6 * z)

    for i in range(6):
        to_sibling(i).wait_recv()

    @pl.when(odd)
    def _():
        for i in range(6):
            for z in range(3):
                put(i, z, in_sib[i, (z + 1) % 2], z >= 1, in_sib[i, 2], 6 * (z + 1))

    @pl.when(jnp.logical_not(odd))
    def _():
        for i in range(6):
            for z in range(3):
                put(i, 7 + z, in_sib[i, z % 2], z >= 2, in_sib[i, 2], 6 * z)

    keep = (lane48 < 64) | ((lane48 < 100) & (t < n_tile - 1)) | ((lane48 >= 100) & (t > 0))
    window_step(V, PV, VM, sides[0], depth, 10, keep)

    @pl.when(s == 0)
    def _():
        VM[0:2] = jnp.zeros((2,) + VM.shape[1:], F32)

    @pl.when(s == n_slab - 1)
    def _():
        VM[6:8] = jnp.zeros((2,) + VM.shape[1:], F32)

    window_step(VM, PV.at[0:8], VH, sides[1], depth.at[1:7], 8, keep)

    @pl.when(s == 0)
    def _():
        VH[0] = jnp.zeros(VH.shape[1:], F32)

    @pl.when(s == n_slab - 1)
    def _():
        VH[5] = jnp.zeros(VH.shape[1:], F32)

    Xf = X.reshape(6 * 64, 128)
    for z in range(6):
        low, mid, top = VH[z, 15:47], 0.75 * VH[z, 16:48], VH[z, 17:49]
        Xf[pl.ds(64 * z, 32, stride=2), :] = 0.25 * low + mid
        Xf[pl.ds(64 * z + 1, 32, stride=2), :] = mid + 0.25 * top

    lane = lanes(64)
    half = lane >> 1
    near = (half + jnp.where((lane & 1) == 1, 1, -1)) & 127
    fine_y, side_y = [], []
    for z in range(6):
        u = lane_pick(X[z], half)
        v = lane_pick(X[z], near)
        fine_y.append(0.75 * u + 0.25 * v)
        side_y.append(0.75 * v + 0.25 * u)

    def at_height(f, zf):
        z = zf // 2
        if zf % 2 == 0:
            return 0.25 * f[z] + 0.75 * f[z + 1]
        return 0.75 * f[z + 1] + 0.25 * f[z + 2]

    def grow(temp, speed, radius):
        under = jnp.maximum(1.0 - temp, 0.0)
        return radius + speed * under * under

    for zf in range(-1, 9):
        if zf == -1:
            sp, ra = face_spd[0], face_rad[0]
        elif zf == 8:
            sp, ra = face_spd[1], face_rad[1]
        else:
            sp, ra = spd[zf], rad[zf]
        Gf[zf + 1, 8:72] = grow(at_height(fine_y, zf), sp, ra)
    for zf in range(8):
        side = grow(at_height(side_y, zf), side_spd[zf], side_rad[zf])
        c = Gf[zf + 1, 8:72]
        near_y = jnp.maximum(
            jnp.where(lane == 0, side, pltpu.roll(c, 1, 1)),
            jnp.where(lane == 127, side, pltpu.roll(c, 127, 1)),
        )
        near_x = jnp.maximum(Gf[zf + 1, 7:71], Gf[zf + 1, 9:73])
        near_z = jnp.maximum(Gf[zf, 8:72], Gf[zf + 2, 8:72])
        env[zf] = jnp.maximum(c, jnp.maximum(jnp.maximum(near_x, near_y), near_z) - 0.5)
    env_copy = pltpu.make_async_copy(env, grown_out, out_sem.at[1])
    env_copy.start()

    for i in range(6):
        to_sibling(i).wait_send()

    n_own = jnp.where(is_source, n_tile - 1, 0) + jnp.where(is_relay, NZ - 1, 0)
    n_out = jnp.where(is_source, n_tile, 0) + jnp.where(is_relay, NZ, 0)

    @pl.loop(0, n_own)
    def _(d):
        send(0, pk_own.at[0], t, 0).wait_send()

    @pl.when(has_outer)
    def _():
        @pl.loop(0, n_out)
        def _(d):
            send(1, pk_out.at[0], t, 0).wait_send()

    heat_copy.wait()
    env_copy.wait()


def local(temperature, spot, labels, radius, position, seeds):
    n_slab, n_tile = lax.axis_size("slab"), lax.axis_size("tile")
    any_spec = pl.BlockSpec(memory_space=pl.ANY)
    vm = pltpu.VMEM
    dma = pltpu.SemaphoreType.DMA
    body = lambda *refs: kernel(n_slab, n_tile, *refs)
    return pl.pallas_call(
        body,
        out_shape=(
            jax.ShapeDtypeStruct((4, 8, 2048), F32),
            jax.ShapeDtypeStruct((8, 64, 128), F32),
        ),
        in_specs=[any_spec] * 6,
        out_specs=(any_spec, any_spec),
        scratch_shapes=[
            vm((4, 8, 2048), F32),
            pltpu.SMEM((2, 2), jnp.int32),
            vm((8, 64, 128), jnp.int32),
            vm((8, 64, 128), F32),
            vm((64,), jnp.int32),
            vm((64,), jnp.int32),
            vm((8, 64, 128), F32),
            vm((8, 12, 16, 128), F32),
            vm((8, 12, 16, 128), F32),
            vm((6, 10, 16, 128), F32),
            vm((4, 8, 16, 128), F32),
            vm((2, 12, 16, 128), F32),
            vm((8, 16, 128), F32),
            vm((32, 3, 8, 128), F32),
            vm((32, 2, 8, 128), F32),
            vm((6, 3, 8, 128), F32),
            vm((6, 2, 8, 128), F32),
            vm((6, 3, 8, 128), F32),
            vm((NZ, 3, 8, 128), F32),
            vm((NZ, 2, 8, 128), F32),
            vm((10, 64, 128), F32),
            vm((10, 64, 128), F32),
            vm((8, 64, 128), F32),
            vm((6, 64, 128), F32),
            vm((6, 64, 128), F32),
            vm((2, 64, 128), F32),
            vm((2, 64, 128), F32),
            vm((8, 512), F32),
            vm((2, 8, 512), F32),
            vm((8, 64, 128), F32),
            vm((8, 64, 128), F32),
            vm((10, 80, 128), F32),
            vm((8, 64, 128), F32),
            dma((6,)),
            dma((2,)),
            dma((14,)),
            dma((14,)),
            dma((2,)),
            dma((3, 6)),
            dma((2, NZ)),
            dma((1,)),
        ],
        compiler_params=pltpu.CompilerParams(collective_id=0, has_side_effects=True),
        name="build_step",
    )(temperature, spot, labels, radius, position, seeds)


def solution(mesh):
    return jax.shard_map(
        local,
        mesh=mesh,
        in_specs=(
            P("slab", "tile", None),
            P(),
            P("slab", None, "tile"),
            P("slab", None, "tile"),
            P(("slab", "tile")),
            P(("slab", "tile")),
        ),
        out_specs=(P("slab", "tile", None), P("slab", None, "tile")),
        check_vma=False,
    )
```

```python
import jax
import jax.numpy as jnp
from jax import lax
from jax.experimental import pallas as pl
from jax.experimental.pallas import tpu as pltpu
from jax.sharding import PartitionSpec as P

HEAT_RATE = 0.1
SOURCE_POWER = 1.5
BEAM_RADIUS_SQ = 36.0
DEPTH_SCALE = 3.0
GOLDEN_ANGLE = 2.39996323
MESH = pl.DeviceIdType.MESH
NZ = 8
FIRST, EARLY = 2, 4
F32 = jnp.float32
NEIGHBOURS = [(a, b) for a in (-1, 0, 1) for b in (-1, 0, 1) if (a, b) != (0, 0)]


def lanes(rows):
    return lax.broadcasted_iota(jnp.int32, (rows, 128), 1)


def lane_pick(x, index):
    return jnp.take_along_axis(x, index, axis=1)


def conductance(v):
    return 0.5 * HEAT_RATE * 1.5 - (0.25 * HEAT_RATE) / (1.0 + v * v)


def next_along_y(x, last):
    r = pltpu.roll(x, 127, 2)
    up = pltpu.roll(r, 15, 1)
    lane = lax.broadcasted_iota(jnp.int32, x.shape, 2)
    row = lax.broadcasted_iota(jnp.int32, x.shape, 1)
    up = jnp.where(row == 15, last, up)
    return jnp.where(lane == 127, up, r)


def before_along_y(x, first):
    r = pltpu.roll(x, 1, 2)
    down = pltpu.roll(r, 1, 1)
    lane = lax.broadcasted_iota(jnp.int32, x.shape, 2)
    row = lax.broadcasted_iota(jnp.int32, x.shape, 1)
    down = jnp.where(row == 0, first, down)
    return jnp.where(lane == 0, down, r)


def heat_step(src, cond, dst, plane, depth, count_z, first_x, last_x, offset_x, fill, unroll):
    wide, inner = slice(first_x, last_x + 2), slice(first_x + 1, last_x + 1)

    def conductances(z, c):
        cond[z, fill] = conductance(src[z, fill])
        return c

    lax.fori_loop(0, count_z, conductances, 0, unroll=unroll)

    def layer(z, c):
        v = src[z + 1, wide]
        p = cond[z + 1, wide]
        flux_x = (p[:-1] + p[1:]) * (v[1:] - v[:-1])
        vc, pc = v[1:-1], p[1:-1]
        total = flux_x[1:] - flux_x[:-1]
        total += (pc + cond[z, inner]) * (src[z, inner] - vc)
        total += (pc + cond[z + 2, inner]) * (src[z + 2, inner] - vc)
        outside = 0.5 * HEAT_RATE
        flux_y = (pc + next_along_y(pc, outside)) * (next_along_y(vc, 0.0) - vc)
        edge = (pc + outside) * vc
        low = jnp.broadcast_to(edge[:, 0:1, 0:1], vc.shape)
        total += flux_y - before_along_y(flux_y, low)
        source = plane[offset_x + first_x : offset_x + last_x] * depth[z]
        dst[z, first_x:last_x] = vc + total + source
        return c

    lax.fori_loop(0, count_z - 2, layer, 0, unroll=unroll)


def window_step(src, cond, dst, plane, depth, count_z, keep):
    for z in range(count_z):
        cond[z] = conductance(src[z])
    for z in range(count_z - 2):
        v, p = src[z + 1, 8:56], cond[z + 1, 8:56]
        total = (p + cond[z, 8:56]) * (src[z, 8:56] - v)
        total += (p + cond[z + 2, 8:56]) * (src[z + 2, 8:56] - v)
        total += (p + cond[z + 1, 7:55]) * (src[z + 1, 7:55] - v)
        total += (p + cond[z + 1, 9:57]) * (src[z + 1, 9:57] - v)
        total += (p + pltpu.roll(p, 1, 1)) * (pltpu.roll(v, 1, 1) - v)
        total += (p + pltpu.roll(p, 127, 1)) * (pltpu.roll(v, 127, 1) - v)
        at = jnp.broadcast_to(depth[z, 0:1, :], v.shape)
        dst[z, 8:56] = jnp.where(keep, v + total + plane * at, 0.0)


def kernel(
    n_slab,
    n_tile,
    x_in,
    spot_in,
    lab_in,
    rad_in,
    pos_in,
    seed_in,
    heat_out,
    grown_out,
    x_v,
    spot,
    lab,
    rad,
    pos,
    seed,
    spd,
    E,
    PE,
    M,
    PM,
    H,
    plane,
    depth,
    pk_own,
    pk_out,
    in_own,
    in_out,
    in_sib,
    rl_own,
    rl_out,
    V,
    PV,
    VM,
    VH,
    X,
    face_rad,
    face_spd,
    cols,
    col_in,
    side_rad,
    side_spd,
    Gf,
    in_sem,
    send_a,
    recv_a,
    send_b,
    recv_b,
    recv_r,
    send_r,
    ready,
    cross,
    side,
):
    s = lax.axis_index("slab")
    t = lax.axis_index("tile")
    first = n_tile // 2 - 3
    sources = tuple(range(first, first + 6))
    is_source = (t >= first) & (t < first + 6)
    n_col = n_tile // NZ
    col, pos_z = t // NZ, t % NZ
    odd = s % 2 == 1
    sib = jnp.where(odd, s - 1, s + 1)
    outer = jnp.where(odd, s + 1, s - 1)
    has_outer = (outer >= 0) & (outer < n_slab)

    def sender_of(q):
        return col * NZ + q % NZ

    relayed = jnp.int32(0)
    is_relay = jnp.bool_(False)
    for i, q in enumerate(sources):
        mine = (pos_z == q % NZ) & ((col != q // NZ))
        relayed = jnp.where(mine, i, relayed)
        is_relay = is_relay | mine

    def there(a, b):
        c = jnp.bool_(True)
        if a == -1:
            c = c & (s > 0)
        if a == 1:
            c = c & (s < n_slab - 1)
        if b == -1:
            c = c & (t > 0)
        if b == 1:
            c = c & (t < n_tile - 1)
        return c

    loads = [
        pltpu.make_async_copy(a, b, in_sem.at[i])
        for i, (a, b) in enumerate(
            (
                (x_in, x_v),
                (lab_in, lab),
                (rad_in, rad),
                (spot_in, spot),
                (pos_in, pos),
                (seed_in, seed),
            )
        )
    ]
    for c in loads:
        c.start()

    late = pos_z >= EARLY
    opens, closes = pos_z == 0, pos_z == NZ - 1
    bar = pltpu.get_barrier_semaphore()
    count = jnp.int32(0)
    crossing = jnp.int32(0)
    for a, b in NEIGHBOURS:
        c = there(a, b)
        later = c & closes if b == 1 else jnp.bool_(False)
        across = c & opens if b == -1 else jnp.bool_(False)

        @pl.when(c & jnp.logical_not(later))
        def _():
            pl.semaphore_signal(bar, inc=1, device_id=(s + a, t + b), device_id_type=MESH)

        count = count + (c & jnp.logical_not(across)).astype(jnp.int32)
        crossing = crossing + across.astype(jnp.int32)
    outer_one = has_outer.astype(jnp.int32)
    for q in sources:
        sender = sender_of(q)

        @pl.when((sender != t) & jnp.logical_not(late))
        def _():
            pl.semaphore_signal(bar, inc=1, device_id=(s, sender), device_id_type=MESH)

        @pl.when(has_outer & jnp.logical_not(late))
        def _():
            pl.semaphore_signal(bar, inc=1, device_id=(outer, sender), device_id_type=MESH)

        count = count + jnp.where(late, (t != sender).astype(jnp.int32) + outer_one, 0)

    def greet_late(column):
        for z in range(EARLY, NZ):
            d = column * NZ + z

            @pl.when(d != t)
            def _():
                pl.semaphore_signal(bar, inc=1, device_id=(s, d), device_id_type=MESH)

            @pl.when(has_outer)
            def _():
                pl.semaphore_signal(bar, inc=1, device_id=(outer, d), device_id_type=MESH)

    @pl.when(is_source)
    def _():
        greet_late(col)

    @pl.when(is_relay)
    def _():
        greet_late(col)

    @pl.when(is_relay)
    def _():
        pl.semaphore_signal(bar, inc=1, device_id=(s, first + relayed), device_id_type=MESH)

    sends = jnp.where(is_source | is_relay, 1, 0)
    me_late = late.astype(jnp.int32)
    n_early = sends * EARLY * (1 + outer_one) - sends * (1 - me_late)
    n_late = sends * (NZ - EARLY) * (1 + outer_one) - sends * me_late
    count = count + n_early + jnp.where(is_source, n_col - 1, 0)

    @pl.when(s == 0)
    def _():
        E[0:2] = jnp.zeros((2,) + E.shape[1:], F32)
        V[0:3] = jnp.zeros((3,) + V.shape[1:], F32)
        face_rad[0] = jnp.zeros((64, 128), F32)
        face_spd[0] = jnp.zeros((64, 128), F32)

    @pl.when(s == n_slab - 1)
    def _():
        E[6:8] = jnp.zeros((2,) + E.shape[1:], F32)
        V[7:10] = jnp.zeros((3,) + V.shape[1:], F32)
        face_rad[1] = jnp.zeros((64, 128), F32)
        face_spd[1] = jnp.zeros((64, 128), F32)

    @pl.when(t == 0)
    def _():
        E[:, 0:2] = jnp.zeros((8, 2) + E.shape[2:], F32)
        col_in[0] = jnp.zeros(col_in.shape[1:], F32)

    @pl.when(t == n_tile - 1)
    def _():
        E[:, 10:12] = jnp.zeros((8, 2) + E.shape[2:], F32)
        col_in[1] = jnp.zeros(col_in.shape[1:], F32)

    loads[0].wait()
    flat = E.reshape(8 * 12 * 16, 128)
    for z in range(4):
        for k in range(16):
            row = ((z + 2) * 12 + 2) * 16 + k
            flat[pl.ds(row, 8, stride=16), :] = x_v[z, :, 128 * k : 128 * k + 128]

    lane8 = lanes(8)
    left = lane8 < 64

    @pl.when(is_source)
    def _():
        def read(z, k):
            if k < 0 or k > 15:
                return jnp.zeros((8, 128), F32)
            return x_v[z, :, 128 * k : 128 * k + 128]

        for k in range(16):
            now = [read(z, k) for z in range(4)]
            turned = [pltpu.roll(v, 64, 1) for v in now]
            h_even = jnp.zeros((8, 128), F32)
            h_odd = jnp.zeros((8, 128), F32)
            for z in range(4):
                low, top = read(z, k - 1), read(z, k + 1)
                here = pltpu.roll(now[z], 67 + 6 * z, 1)
                low = pltpu.roll(low, 3 + 6 * z, 1)
                top = pltpu.roll(top, 3 + 6 * z, 1)
                one = (lane8 >= 6 * z) & (lane8 < 6 * z + 3)
                two = (lane8 >= 6 * z + 3) & (lane8 < 6 * z + 6)
                h_even = jnp.where(one, low, jnp.where(two, here, h_even))
                h_odd = jnp.where(one, here, jnp.where(two, top, h_odd))
            for parity, lo, up, halo in ((0, now, turned, h_even), (1, turned, now, h_odd)):
                d = 2 * k + parity
                far = pltpu.roll(halo, 64, 1)
                pk_own[d, 0] = jnp.where(left, lo[0], up[2])
                pk_own[d, 1] = jnp.where(left, lo[1], up[3])
                pk_own[d, 2] = halo
                pk_out[d, 0] = jnp.where(
                    left, jnp.where(odd, lo[1], lo[0]), jnp.where(odd, up[2], up[1])
                )
                pk_out[d, 1] = jnp.where(left, jnp.where(odd, lo[3], lo[2]), far)

    hi = lax.Precision.HIGHEST
    pick_r = lax.broadcasted_iota(jnp.int32, (8, 128), 0)
    lane48 = lanes(48)
    wy = t * 64 + lane48 - jnp.where(lane48 < 100, 0, 128)
    wx = lax.broadcasted_iota(jnp.int32, (48, 128), 0) + first * 8
    def prepare():
        for c in loads[1:]:
            c.wait()
        place = pos[...].reshape(1, 64)
        value = ((seed[...].reshape(1, 64) & 63) + 1).astype(F32)
        rows = lax.broadcasted_iota(jnp.int32, (512, 64), 0)
        cells = lax.broadcasted_iota(jnp.int32, (128, 64), 0)
        in_row = jnp.where(rows == (place >> 7), 1.0, 0.0).astype(jnp.bfloat16)
        in_lane = jnp.where(cells == (place & 127), value, 0.0).astype(jnp.bfloat16)
        named = lax.dot_general(
            in_row, in_lane, (((1,), (1,)), ((), ())), preferred_element_type=F32
        ).reshape(8, 64, 128)
        theta = GOLDEN_ANGLE * lanes(8).astype(F32)
        table = 1.0 + 0.5 * jnp.cos(4.0 * theta)
        table = jnp.broadcast_to(table[0:1], (64, 128))
        for z in range(8):
            grain = jnp.where(named[z] > 0.5, named[z].astype(jnp.int32) - 1, lab[z] & 63)
            spd[z] = lane_pick(table, grain)

        nt = (((1,), (1,)), ((), ()))
        e_rad = jnp.where(
            ((pick_r == 0) & (lane8 == 127)) | ((pick_r == 2) & (lane8 == 0)), 1.0, 0.0
        )
        e_spd = jnp.where(
            ((pick_r == 1) & (lane8 == 127)) | ((pick_r == 3) & (lane8 == 0)), 1.0, 0.0
        )
        cols[...] = lax.dot_general(
            e_rad, rad[...].reshape(512, 128), nt, precision=hi, preferred_element_type=F32
        ) + lax.dot_general(
            e_spd, spd[...].reshape(512, 128), nt, precision=hi, preferred_element_type=F32
        )

        for step in range(2):
            row = lax.broadcasted_iota(jnp.int32, (12, 16, 128), 0)
            y = lax.broadcasted_iota(jnp.int32, (12, 16, 128), 1) * 128
            y = y + lax.broadcasted_iota(jnp.int32, (12, 16, 128), 2)
            xd = (t * 8 - 2 + row - spot[step, 0]).astype(F32)
            yd = (y - spot[step, 1]).astype(F32)
            plane[step] = SOURCE_POWER * jnp.exp(-(xd * xd + yd * yd) / BEAM_RADIUS_SQ)
            xd = (wx - spot[step, 0]).astype(F32)
            yd = (wy - spot[step, 1]).astype(F32)
            side[step] = SOURCE_POWER * jnp.exp(-(xd * xd + yd * yd) / BEAM_RADIUS_SQ)
        level = lax.broadcasted_iota(jnp.int32, (8, 16, 128), 0) + (s * 4 - 2)
        depth[...] = jnp.exp(-(n_slab * 4 - 1 - level).astype(F32) / DEPTH_SCALE)


    @pl.when(jnp.logical_not(late))
    def _():
        prepare()

    pl.semaphore_wait(bar, count)

    halos = []
    for a, b in NEIGHBOURS:
        zs = {0: (2, 4, 2), -1: (2, 2, 6), 1: (4, 2, 0)}[a]
        xs = {0: (2, 8, 2), -1: (2, 2, 10), 1: (8, 2, 0)}[b]
        if a != 0 and b != 0:
            zs = {-1: (2, 1, 6), 1: (5, 1, 1)}[a]
            xs = {-1: (2, 1, 10), 1: (9, 1, 1)}[b]
        k = len(halos)
        halos.append(
            (
                a,
                b,
                pltpu.make_async_remote_copy(
                    src_ref=E.at[pl.ds(zs[0], zs[1]), pl.ds(xs[0], xs[1])],
                    dst_ref=E.at[pl.ds(zs[2], zs[1]), pl.ds(xs[2], xs[1])],
                    send_sem=send_a.at[k],
                    recv_sem=recv_a.at[k],
                    device_id=(s + a, t + b),
                    device_id_type=MESH,
                ),
            )
        )
    def now(a, b):
        return there(a, b) & jnp.logical_not(opens) if b == -1 else there(a, b)

    def send_halos():
        for a, b, copy in sorted(halos, key=lambda h: -h[1]):

            @pl.when(now(a, b))
            def _():
                copy.start()

    for a in (-1, 0, 1):

        @pl.when(there(a, 1) & closes)
        def _():
            pl.semaphore_signal(cross, inc=1, device_id=(s + a, t + 1), device_id_type=MESH)

    @pl.when(jnp.logical_not(is_source))
    def _():
        send_halos()

    for q in sources:
        sender = sender_of(q)

        @pl.when(late & (sender != t))
        def _():
            pl.semaphore_signal(ready, inc=1, device_id=(s, sender), device_id_type=MESH)

        @pl.when(late & has_outer)
        def _():
            pl.semaphore_signal(ready, inc=1, device_id=(outer, sender), device_id_type=MESH)

    def send(kind, src, d, i):
        own = jnp.int32(i) if isinstance(i, int) else i
        return pltpu.make_async_remote_copy(
            src_ref=src,
            dst_ref=(in_own, in_out)[kind].at[own],
            send_sem=send_b.at[kind],
            recv_sem=recv_b.at[kind, own],
            device_id=((s, outer)[kind], d),
            device_id_type=MESH,
        )

    def to_relay(kind, d, at, z):
        return pltpu.make_async_remote_copy(
            src_ref=(pk_own, pk_out)[kind].at[d],
            dst_ref=(rl_own, rl_out)[kind].at[z],
            send_sem=send_b.at[kind],
            recv_sem=recv_r.at[kind, z],
            device_id=(s, at),
            device_id_type=MESH,
        )

    def to_sibling(i):
        return pltpu.make_async_remote_copy(
            src_ref=in_own.at[i],
            dst_ref=in_sib.at[i],
            send_sem=send_r.at[0],
            recv_sem=recv_b.at[2, i],
            device_id=(sib, t),
            device_id_type=MESH,
        )

    own_slot = t - first

    def relay_columns(z):
        for c in (1, n_col - 1) + tuple(range(2, n_col - 1)):
            d = (col + c) % n_col * NZ + z
            at = (col + c) % n_col * NZ + pos_z
            to_relay(0, d, at, z).start()

            @pl.when(has_outer)
            def _():
                to_relay(1, d, at, z).start()

    def direct_columns(z):
        d = col * NZ + z

        @pl.when(d != t)
        def _():
            send(0, pk_own.at[d], d, own_slot).start()

        @pl.when(has_outer)
        def _():
            send(1, pk_out.at[d], d, own_slot).start()

    @pl.when(is_source)
    def _():
        @pl.loop(0, FIRST)
        def _(z):
            relay_columns(z)
            direct_columns(z)

        send_halos()

        in_own[own_slot] = pk_own[t]

    @pl.when(late)
    def _():
        prepare()

    fine = []
    k0 = len(NEIGHBOURS)
    for a, z in ((1, 7), (-1, 0)):
        slot = 0 if a == 1 else 1
        fine.append((a, 0, rad.at[z], face_rad.at[slot], (s + a, t)))
        fine.append((a, 0, spd.at[z], face_spd.at[slot], (s + a, t)))
    for b in (1, -1):
        slot = 0 if b == 1 else 1
        fine.append((0, b, cols, col_in.at[slot], (s, t + b)))
    fine = [
        (
            a,
            b,
            pltpu.make_async_remote_copy(
                src_ref=src,
                dst_ref=dst,
                send_sem=send_a.at[k0 + i],
                recv_sem=recv_a.at[k0 + i],
                device_id=to,
                device_id_type=MESH,
            ),
        )
        for i, (a, b, src, dst, to) in enumerate(fine)
    ]
    for a, b, copy in fine:

        @pl.when(now(a, b))
        def _():
            copy.start()

    @pl.when(is_source)
    def _():
        @pl.loop(FIRST, EARLY)
        def _(z):
            relay_columns(z)
            direct_columns(z)

        @pl.loop(EARLY, NZ)
        def _(z):
            relay_columns(z)

    def await_halos(before):
        for a, b, copy in halos:
            if (b == 1) == before:

                @pl.when(there(-a, -b))
                def _():
                    copy.wait_recv()

    def edges_of_step():
        @pl.when(s == 0)
        def _():
            M[0:1] = jnp.zeros((1,) + M.shape[1:], F32)

        @pl.when(s == n_slab - 1)
        def _():
            M[5:6] = jnp.zeros((1,) + M.shape[1:], F32)

        @pl.when(t == 0)
        def _():
            M[:, 0:1] = jnp.zeros((6, 1) + M.shape[2:], F32)

        @pl.when(t == n_tile - 1)
        def _():
            M[:, 9:10] = jnp.zeros((6, 1) + M.shape[2:], F32)

    def first_part():
        await_halos(False)
        heat_step(E, PE, M, plane.at[0], depth.at[1:7], 8, 2, 10, 1, slice(2, 12), False)
        edges_of_step()
        heat_step(M, PM, H, plane.at[1], depth.at[2:6], 6, 2, 8, 2, slice(2, 10), False)

    @pl.when(jnp.logical_not(late))
    def _():
        first_part()

    def forward(z):
        d = col * NZ + z
        to_relay(0, d, t, z).wait_recv()

        @pl.when(d != t)
        def _():
            send(0, rl_own.at[z], d, relayed).start()

        @pl.when(d == t)
        def _():
            in_own[relayed] = rl_own[z]

        @pl.when(has_outer)
        def _():
            to_relay(1, d, t, z).wait_recv()
            send(1, rl_out.at[z], d, relayed).start()

    @pl.when(is_relay)
    def _():
        @pl.loop(0, EARLY)
        def _(z):
            forward(z)

    @pl.when(opens & (t > 0))
    def _():
        pl.semaphore_wait(cross, crossing)
        for a, b, copy in halos + fine:
            if b == -1:

                @pl.when(there(a, b))
                def _():
                    copy.start()

    @pl.when(sends > 0)
    def _():
        pl.semaphore_wait(ready, n_late)

    @pl.when(is_source)
    def _():
        @pl.loop(EARLY, NZ)
        def _(z):
            direct_columns(z)

    @pl.when(is_relay)
    def _():
        @pl.loop(EARLY, NZ)
        def _(z):
            forward(z)

    @pl.when(late)
    def _():
        first_part()

    for a, b, copy in fine:

        @pl.when(there(-a, -b))
        def _():
            copy.wait_recv()

    for a, b, copy in fine:

        @pl.when(there(a, b))
        def _():
            copy.wait_send()

    r16 = lax.broadcasted_iota(jnp.int32, (16, 128), 0)
    l16 = lanes(16)
    both = col_in[...].reshape(16, 512)
    tn = (((0,), (0,)), ((), ()))
    s_rad = jnp.where(((r16 == 0) & (l16 == 0)) | ((r16 == 10) & (l16 == 127)), 1.0, 0.0)
    s_spd = jnp.where(((r16 == 1) & (l16 == 0)) | ((r16 == 11) & (l16 == 127)), 1.0, 0.0)
    side_rad[...] = lax.dot_general(
        both, s_rad, tn, precision=hi, preferred_element_type=F32
    ).reshape(8, 64, 128)
    side_spd[...] = lax.dot_general(
        both, s_spd, tn, precision=hi, preferred_element_type=F32
    ).reshape(8, 64, 128)
    for z in range(10):
        Gf[z, 0:8] = jnp.zeros((8, 128), F32)
        Gf[z, 72:80] = jnp.zeros((8, 128), F32)

    await_halos(True)
    heat_step(E, PE, M, plane.at[0], depth.at[1:7], 8, 0, 2, 1, slice(0, 2), True)
    edges_of_step()
    heat_step(M, PM, H, plane.at[1], depth.at[2:6], 6, 0, 2, 2, slice(0, 2), True)

    Hf = H.reshape(4 * 8 * 16, 128)
    for z in range(4):
        for k in range(16):
            heat_out[z, :, 128 * k : 128 * k + 128] = Hf[pl.ds(z * 128 + k, 8, stride=16), :]

    for i, q in enumerate(sources):

        @pl.when(sender_of(q) != t)
        def _():
            send(0, pk_own.at[0], t, i).wait_recv()

        to_sibling(i).start()

        @pl.when(has_outer)
        def _():
            send(1, pk_out.at[0], t, i).wait_recv()

    far_lane = jnp.where(lane8 >= 100, lane8 - 125, lane8 - 61)

    def put(i, z, tile, high, halo, base):
        body = pltpu.roll(tile, 64, 1) if high else tile
        around = lane_pick(halo, (far_lane + base) & 127)
        V[z, 8 + 8 * i : 16 + 8 * i] = jnp.where(left, body, around)

    for i in range(6):
        for z in range(4):
            put(i, 3 + z, in_own[i, z % 2], z >= 2, in_own[i, 2], 6 * z)

    @pl.when(has_outer)
    def _():
        at = jnp.where(odd, 7, 0)
        base = 64 + jnp.where(odd, 0, 6)
        for i in range(6):
            for z in range(3):
                put(i, at + z, in_out[i, z // 2], z == 1, in_out[i, 1], base + 6 * z)

    for i in range(6):
        to_sibling(i).wait_recv()

    @pl.when(odd)
    def _():
        for i in range(6):
            for z in range(3):
                put(i, z, in_sib[i, (z + 1) % 2], z >= 1, in_sib[i, 2], 6 * (z + 1))

    @pl.when(jnp.logical_not(odd))
    def _():
        for i in range(6):
            for z in range(3):
                put(i, 7 + z, in_sib[i, z % 2], z >= 2, in_sib[i, 2], 6 * z)

    keep = (lane48 < 64) | ((lane48 < 100) & (t < n_tile - 1)) | ((lane48 >= 100) & (t > 0))
    window_step(V, PV, VM, side[0], depth, 10, keep)

    @pl.when(s == 0)
    def _():
        VM[0:2] = jnp.zeros((2,) + VM.shape[1:], F32)

    @pl.when(s == n_slab - 1)
    def _():
        VM[6:8] = jnp.zeros((2,) + VM.shape[1:], F32)

    window_step(VM, PV.at[0:8], VH, side[1], depth.at[1:7], 8, keep)

    @pl.when(s == 0)
    def _():
        VH[0] = jnp.zeros(VH.shape[1:], F32)

    @pl.when(s == n_slab - 1)
    def _():
        VH[5] = jnp.zeros(VH.shape[1:], F32)

    Xf = X.reshape(6 * 64, 128)
    for z in range(6):
        low, mid, top = VH[z, 15:47], 0.75 * VH[z, 16:48], VH[z, 17:49]
        Xf[pl.ds(64 * z, 32, stride=2), :] = 0.25 * low + mid
        Xf[pl.ds(64 * z + 1, 32, stride=2), :] = mid + 0.25 * top

    lane = lanes(64)
    half = lane >> 1
    near = (half + jnp.where((lane & 1) == 1, 1, -1)) & 127
    fine_y, side_y = [], []
    for z in range(6):
        u = lane_pick(X[z], half)
        v = lane_pick(X[z], near)
        fine_y.append(0.75 * u + 0.25 * v)
        side_y.append(0.75 * v + 0.25 * u)

    def at_height(f, zf):
        z = zf // 2
        if zf % 2 == 0:
            return 0.25 * f[z] + 0.75 * f[z + 1]
        return 0.75 * f[z + 1] + 0.25 * f[z + 2]

    def grow(temp, speed, radius):
        under = jnp.maximum(1.0 - temp, 0.0)
        return radius + speed * under * under

    for zf in range(-1, 9):
        if zf == -1:
            sp, ra = face_spd[0], face_rad[0]
        elif zf == 8:
            sp, ra = face_spd[1], face_rad[1]
        else:
            sp, ra = spd[zf], rad[zf]
        Gf[zf + 1, 8:72] = grow(at_height(fine_y, zf), sp, ra)
    for zf in range(8):
        side = grow(at_height(side_y, zf), side_spd[zf], side_rad[zf])
        c = Gf[zf + 1, 8:72]
        near_y = jnp.maximum(
            jnp.where(lane == 0, side, pltpu.roll(c, 1, 1)),
            jnp.where(lane == 127, side, pltpu.roll(c, 127, 1)),
        )
        near_x = jnp.maximum(Gf[zf + 1, 7:71], Gf[zf + 1, 9:73])
        near_z = jnp.maximum(Gf[zf, 8:72], Gf[zf + 2, 8:72])
        grown_out[zf] = jnp.maximum(c, jnp.maximum(jnp.maximum(near_x, near_y), near_z) - 0.5)
    for a, b, copy in halos:

        @pl.when(there(a, b))
        def _():
            copy.wait_send()

    for i in range(6):
        to_sibling(i).wait_send()

    n_own = jnp.where(is_source, n_tile - 1, 0) + jnp.where(is_relay, NZ - 1, 0)
    n_out = jnp.where(is_source, n_tile, 0) + jnp.where(is_relay, NZ, 0)

    @pl.loop(0, n_own)
    def _(d):
        send(0, pk_own.at[0], t, 0).wait_send()

    @pl.when(has_outer)
    def _():
        @pl.loop(0, n_out)
        def _(d):
            send(1, pk_out.at[0], t, 0).wait_send()


def local(temperature, spot, labels, radius, position, seeds):
    n_slab, n_tile = lax.axis_size("slab"), lax.axis_size("tile")
    any_spec = pl.BlockSpec(memory_space=pl.ANY)
    vm = pltpu.VMEM
    dma = pltpu.SemaphoreType.DMA
    body = lambda *refs: kernel(n_slab, n_tile, *refs)
    return pl.pallas_call(
        body,
        out_shape=(
            vm((4, 8, 2048), F32),
            vm((8, 64, 128), F32),
        ),
        in_specs=[any_spec] * 6,
        out_specs=(pl.BlockSpec(memory_space=pltpu.VMEM),) * 2,
        scratch_shapes=[
            vm((4, 8, 2048), F32),
            pltpu.SMEM((2, 2), jnp.int32),
            vm((8, 64, 128), jnp.int32),
            vm((8, 64, 128), F32),
            vm((64,), jnp.int32),
            vm((64,), jnp.int32),
            vm((8, 64, 128), F32),
            vm((8, 12, 16, 128), F32),
            vm((8, 12, 16, 128), F32),
            vm((6, 10, 16, 128), F32),
            vm((6, 10, 16, 128), F32),
            vm((4, 8, 16, 128), F32),
            vm((2, 12, 16, 128), F32),
            vm((8, 16, 128), F32),
            vm((32, 3, 8, 128), F32),
            vm((32, 2, 8, 128), F32),
            vm((6, 3, 8, 128), F32),
            vm((6, 2, 8, 128), F32),
            vm((6, 3, 8, 128), F32),
            vm((NZ, 3, 8, 128), F32),
            vm((NZ, 2, 8, 128), F32),
            vm((10, 64, 128), F32),
            vm((10, 64, 128), F32),
            vm((8, 64, 128), F32),
            vm((6, 64, 128), F32),
            vm((6, 64, 128), F32),
            vm((2, 64, 128), F32),
            vm((2, 64, 128), F32),
            vm((8, 512), F32),
            vm((2, 8, 512), F32),
            vm((8, 64, 128), F32),
            vm((8, 64, 128), F32),
            vm((10, 80, 128), F32),
            dma((6,)),
            dma((14,)),
            dma((14,)),
            dma((2,)),
            dma((3, 6)),
            dma((2, NZ)),
            dma((1,)),
            pltpu.SemaphoreType.REGULAR,
            pltpu.SemaphoreType.REGULAR,
            vm((2, 48, 128), F32),
        ],
        compiler_params=pltpu.CompilerParams(collective_id=0, has_side_effects=True),
        name="build_step",
    )(temperature, spot, labels, radius, position, seeds)


def solution(mesh):
    return jax.shard_map(
        local,
        mesh=mesh,
        in_specs=(
            P("slab", "tile", None),
            P(),
            P("slab", None, "tile"),
            P("slab", None, "tile"),
            P(("slab", "tile")),
            P(("slab", "tile")),
        ),
        out_specs=(P("slab", "tile", None), P("slab", None, "tile")),
        check_vma=False,
    )
```

```python
import jax
import jax.numpy as jnp
from jax import lax
from jax.experimental import pallas as pl
from jax.experimental.pallas import tpu as pltpu
from jax.sharding import PartitionSpec as P

HEAT_RATE = 0.1
SOURCE_POWER = 1.5
BEAM_RADIUS_SQ = 36.0
DEPTH_SCALE = 3.0
GOLDEN_ANGLE = 2.39996323
MESH = pl.DeviceIdType.MESH
NZ = 8
FIRST, EARLY = 2, 4
F32 = jnp.float32
NEIGHBOURS = [(a, b) for a in (-1, 0, 1) for b in (-1, 0, 1) if (a, b) != (0, 0)]


def lanes(rows):
    return lax.broadcasted_iota(jnp.int32, (rows, 128), 1)


def lane_pick(x, index):
    return jnp.take_along_axis(x, index, axis=1)


def conductance(v):
    return 0.5 * HEAT_RATE * 1.5 - (0.25 * HEAT_RATE) / (1.0 + v * v)


def next_along_y(x, last):
    r = pltpu.roll(x, 127, 2)
    up = pltpu.roll(r, 15, 1)
    lane = lax.broadcasted_iota(jnp.int32, x.shape, 2)
    row = lax.broadcasted_iota(jnp.int32, x.shape, 1)
    up = jnp.where(row == 15, last, up)
    return jnp.where(lane == 127, up, r)


def before_along_y(x, first):
    r = pltpu.roll(x, 1, 2)
    down = pltpu.roll(r, 1, 1)
    lane = lax.broadcasted_iota(jnp.int32, x.shape, 2)
    row = lax.broadcasted_iota(jnp.int32, x.shape, 1)
    down = jnp.where(row == 0, first, down)
    return jnp.where(lane == 0, down, r)


def heat_step(src, cond, dst, plane, depth, count_z, first_x, last_x, offset_x, fill, unroll):
    wide, inner = slice(first_x, last_x + 2), slice(first_x + 1, last_x + 1)

    def conductances(z, c):
        cond[z, fill] = conductance(src[z, fill])
        return c

    lax.fori_loop(0, count_z, conductances, 0, unroll=unroll)

    def layer(z, c):
        v = src[z + 1, wide]
        p = cond[z + 1, wide]
        flux_x = (p[:-1] + p[1:]) * (v[1:] - v[:-1])
        vc, pc = v[1:-1], p[1:-1]
        total = flux_x[1:] - flux_x[:-1]
        total += (pc + cond[z, inner]) * (src[z, inner] - vc)
        total += (pc + cond[z + 2, inner]) * (src[z + 2, inner] - vc)
        outside = 0.5 * HEAT_RATE
        flux_y = (pc + next_along_y(pc, outside)) * (next_along_y(vc, 0.0) - vc)
        edge = (pc + outside) * vc
        low = jnp.broadcast_to(edge[:, 0:1, 0:1], vc.shape)
        total += flux_y - before_along_y(flux_y, low)
        source = plane[offset_x + first_x : offset_x + last_x] * depth[z]
        dst[z, first_x:last_x] = vc + total + source
        return c

    lax.fori_loop(0, count_z - 2, layer, 0, unroll=unroll)


def window_step(src, cond, dst, plane, depth, count_z, keep):
    for z in range(count_z):
        cond[z] = conductance(src[z])
    for z in range(count_z - 2):
        v, p = src[z + 1, 8:56], cond[z + 1, 8:56]
        total = (p + cond[z, 8:56]) * (src[z, 8:56] - v)
        total += (p + cond[z + 2, 8:56]) * (src[z + 2, 8:56] - v)
        total += (p + cond[z + 1, 7:55]) * (src[z + 1, 7:55] - v)
        total += (p + cond[z + 1, 9:57]) * (src[z + 1, 9:57] - v)
        total += (p + pltpu.roll(p, 1, 1)) * (pltpu.roll(v, 1, 1) - v)
        total += (p + pltpu.roll(p, 127, 1)) * (pltpu.roll(v, 127, 1) - v)
        at = jnp.broadcast_to(depth[z, 0:1, :], v.shape)
        dst[z, 8:56] = jnp.where(keep, v + total + plane * at, 0.0)


def kernel(
    n_slab,
    n_tile,
    x_in,
    spot_in,
    lab_in,
    rad_in,
    pos_in,
    seed_in,
    heat_out,
    grown_out,
    x_v,
    spot,
    lab,
    rad,
    pos,
    seed,
    spd,
    E,
    PE,
    M,
    PM,
    H,
    plane,
    depth,
    pk_own,
    pk_out,
    in_own,
    in_out,
    in_sib,
    rl_own,
    rl_out,
    V,
    PV,
    VM,
    VH,
    X,
    face_rad,
    face_spd,
    cols,
    col_in,
    side_rad,
    side_spd,
    Gf,
    in_sem,
    send_a,
    recv_a,
    send_b,
    recv_b,
    recv_r,
    send_r,
    ready,
    cross,
    side,
):
    s = lax.axis_index("slab")
    t = lax.axis_index("tile")
    first = n_tile // 2 - 3
    sources = tuple(range(first, first + 6))
    is_source = (t >= first) & (t < first + 6)
    n_col = n_tile // NZ
    col, pos_z = t // NZ, t % NZ
    odd = s % 2 == 1
    sib = jnp.where(odd, s - 1, s + 1)
    outer = jnp.where(odd, s + 1, s - 1)
    has_outer = (outer >= 0) & (outer < n_slab)

    def sender_of(q):
        return col * NZ + q % NZ

    relayed = jnp.int32(0)
    is_relay = jnp.bool_(False)
    for i, q in enumerate(sources):
        mine = (pos_z == q % NZ) & ((col != q // NZ))
        relayed = jnp.where(mine, i, relayed)
        is_relay = is_relay | mine

    def there(a, b):
        c = jnp.bool_(True)
        if a == -1:
            c = c & (s > 0)
        if a == 1:
            c = c & (s < n_slab - 1)
        if b == -1:
            c = c & (t > 0)
        if b == 1:
            c = c & (t < n_tile - 1)
        return c

    bar = pltpu.get_barrier_semaphore()

    @pl.when(is_relay)
    def _():
        pl.semaphore_signal(bar, inc=1, device_id=(s, first + relayed), device_id_type=MESH)

    outer_one = has_outer.astype(jnp.int32)

    @pl.when(is_source | is_relay)
    def _():
        for z in range(EARLY, NZ):
            d = col * NZ + z
            apart = jnp.abs(pos_z - z) > 1

            @pl.when(apart)
            def _():
                pl.semaphore_signal(bar, inc=1, device_id=(s, d), device_id_type=MESH)

            @pl.when(apart & has_outer)
            def _():
                pl.semaphore_signal(bar, inc=1, device_id=(outer, d), device_id_type=MESH)

    loads = [
        pltpu.make_async_copy(a, b, in_sem.at[i])
        for i, (a, b) in enumerate(
            (
                (x_in, x_v),
                (lab_in, lab),
                (rad_in, rad),
                (spot_in, spot),
                (pos_in, pos),
                (seed_in, seed),
            )
        )
    ]
    for c in loads:
        c.start()

    late = pos_z >= EARLY
    opens, closes = pos_z == 0, pos_z == NZ - 1
    count = jnp.int32(0)
    crossing = jnp.int32(0)
    for a, b in NEIGHBOURS:
        c = there(a, b)
        later = c & closes if b == 1 else jnp.bool_(False)
        across = c & opens if b == -1 else jnp.bool_(False)

        @pl.when(c & jnp.logical_not(later))
        def _():
            pl.semaphore_signal(bar, inc=1, device_id=(s + a, t + b), device_id_type=MESH)

        count = count + (c & jnp.logical_not(across)).astype(jnp.int32)
        crossing = crossing + across.astype(jnp.int32)
    for q in sources:
        sender = sender_of(q)

        @pl.when((sender != t) & jnp.logical_not(late))
        def _():
            pl.semaphore_signal(bar, inc=1, device_id=(s, sender), device_id_type=MESH)

        @pl.when(has_outer & jnp.logical_not(late))
        def _():
            pl.semaphore_signal(bar, inc=1, device_id=(outer, sender), device_id_type=MESH)

        apart = jnp.abs(pos_z - q % NZ) > 1
        count = count + jnp.where(late & apart, 1 + outer_one, 0)

    sends = jnp.where(is_source | is_relay, 1, 0)
    me_late = late.astype(jnp.int32)
    n_early = sends * EARLY * (1 + outer_one) - sends * (1 - me_late)
    n_late = sends * (NZ - EARLY) * (1 + outer_one) - sends * me_late
    count = count + n_early + jnp.where(is_source, n_col - 1, 0)

    @pl.when(s == 0)
    def _():
        E[0:2] = jnp.zeros((2,) + E.shape[1:], F32)
        V[0:3] = jnp.zeros((3,) + V.shape[1:], F32)
        face_rad[0] = jnp.zeros((64, 128), F32)
        face_spd[0] = jnp.zeros((64, 128), F32)

    @pl.when(s == n_slab - 1)
    def _():
        E[6:8] = jnp.zeros((2,) + E.shape[1:], F32)
        V[7:10] = jnp.zeros((3,) + V.shape[1:], F32)
        face_rad[1] = jnp.zeros((64, 128), F32)
        face_spd[1] = jnp.zeros((64, 128), F32)

    @pl.when(t == 0)
    def _():
        E[:, 0:2] = jnp.zeros((8, 2) + E.shape[2:], F32)
        col_in[0] = jnp.zeros(col_in.shape[1:], F32)

    @pl.when(t == n_tile - 1)
    def _():
        E[:, 10:12] = jnp.zeros((8, 2) + E.shape[2:], F32)
        col_in[1] = jnp.zeros(col_in.shape[1:], F32)

    loads[0].wait()
    flat = E.reshape(8 * 12 * 16, 128)
    for z in range(4):
        for k in range(16):
            row = ((z + 2) * 12 + 2) * 16 + k
            flat[pl.ds(row, 8, stride=16), :] = x_v[z, :, 128 * k : 128 * k + 128]

    lane8 = lanes(8)
    left = lane8 < 64

    @pl.when(is_source)
    def _():
        def read(z, k):
            if k < 0 or k > 15:
                return jnp.zeros((8, 128), F32)
            return x_v[z, :, 128 * k : 128 * k + 128]

        for k in range(16):
            now = [read(z, k) for z in range(4)]
            turned = [pltpu.roll(v, 64, 1) for v in now]
            h_even = jnp.zeros((8, 128), F32)
            h_odd = jnp.zeros((8, 128), F32)
            for z in range(4):
                low, top = read(z, k - 1), read(z, k + 1)
                here = pltpu.roll(now[z], 67 + 6 * z, 1)
                low = pltpu.roll(low, 3 + 6 * z, 1)
                top = pltpu.roll(top, 3 + 6 * z, 1)
                one = (lane8 >= 6 * z) & (lane8 < 6 * z + 3)
                two = (lane8 >= 6 * z + 3) & (lane8 < 6 * z + 6)
                h_even = jnp.where(one, low, jnp.where(two, here, h_even))
                h_odd = jnp.where(one, here, jnp.where(two, top, h_odd))
            for parity, lo, up, halo in ((0, now, turned, h_even), (1, turned, now, h_odd)):
                d = 2 * k + parity
                far = pltpu.roll(halo, 64, 1)
                pk_own[d, 0] = jnp.where(left, lo[0], up[2])
                pk_own[d, 1] = jnp.where(left, lo[1], up[3])
                pk_own[d, 2] = halo
                pk_out[d, 0] = jnp.where(
                    left, jnp.where(odd, lo[1], lo[0]), jnp.where(odd, up[2], up[1])
                )
                pk_out[d, 1] = jnp.where(left, jnp.where(odd, lo[3], lo[2]), far)

    hi = lax.Precision.HIGHEST
    pick_r = lax.broadcasted_iota(jnp.int32, (8, 128), 0)
    lane48 = lanes(48)
    wy = t * 64 + lane48 - jnp.where(lane48 < 100, 0, 128)
    wx = lax.broadcasted_iota(jnp.int32, (48, 128), 0) + first * 8
    def prepare():
        for c in loads[1:]:
            c.wait()
        place = pos[...].reshape(1, 64)
        value = ((seed[...].reshape(1, 64) & 63) + 1).astype(F32)
        rows = lax.broadcasted_iota(jnp.int32, (512, 64), 0)
        cells = lax.broadcasted_iota(jnp.int32, (128, 64), 0)
        in_row = jnp.where(rows == (place >> 7), 1.0, 0.0).astype(jnp.bfloat16)
        in_lane = jnp.where(cells == (place & 127), value, 0.0).astype(jnp.bfloat16)
        named = lax.dot_general(
            in_row, in_lane, (((1,), (1,)), ((), ())), preferred_element_type=F32
        ).reshape(8, 64, 128)
        theta = GOLDEN_ANGLE * lanes(8).astype(F32)
        table = 1.0 + 0.5 * jnp.cos(4.0 * theta)
        table = jnp.broadcast_to(table[0:1], (64, 128))
        for z in range(8):
            grain = jnp.where(named[z] > 0.5, named[z].astype(jnp.int32) - 1, lab[z] & 63)
            spd[z] = lane_pick(table, grain)

        nt = (((1,), (1,)), ((), ()))
        e_rad = jnp.where(
            ((pick_r == 0) & (lane8 == 127)) | ((pick_r == 2) & (lane8 == 0)), 1.0, 0.0
        )
        e_spd = jnp.where(
            ((pick_r == 1) & (lane8 == 127)) | ((pick_r == 3) & (lane8 == 0)), 1.0, 0.0
        )
        cols[...] = lax.dot_general(
            e_rad, rad[...].reshape(512, 128), nt, precision=hi, preferred_element_type=F32
        ) + lax.dot_general(
            e_spd, spd[...].reshape(512, 128), nt, precision=hi, preferred_element_type=F32
        )

    def prepare_beam():
        for step in range(2):
            row = lax.broadcasted_iota(jnp.int32, (12, 16, 128), 0)
            y = lax.broadcasted_iota(jnp.int32, (12, 16, 128), 1) * 128
            y = y + lax.broadcasted_iota(jnp.int32, (12, 16, 128), 2)
            xd = (t * 8 - 2 + row - spot[step, 0]).astype(F32)
            yd = (y - spot[step, 1]).astype(F32)
            plane[step] = SOURCE_POWER * jnp.exp(-(xd * xd + yd * yd) / BEAM_RADIUS_SQ)
            xd = (wx - spot[step, 0]).astype(F32)
            yd = (wy - spot[step, 1]).astype(F32)
            side[step] = SOURCE_POWER * jnp.exp(-(xd * xd + yd * yd) / BEAM_RADIUS_SQ)
        level = lax.broadcasted_iota(jnp.int32, (8, 16, 128), 0) + (s * 4 - 2)
        depth[...] = jnp.exp(-(n_slab * 4 - 1 - level).astype(F32) / DEPTH_SCALE)


    @pl.when(jnp.logical_not(late))
    def _():
        prepare()
        prepare_beam()

    pl.semaphore_wait(bar, count)

    halos = []
    for a, b in NEIGHBOURS:
        zs = {0: (2, 4, 2), -1: (2, 2, 6), 1: (4, 2, 0)}[a]
        xs = {0: (2, 8, 2), -1: (2, 2, 10), 1: (8, 2, 0)}[b]
        if a != 0 and b != 0:
            zs = {-1: (2, 1, 6), 1: (5, 1, 1)}[a]
            xs = {-1: (2, 1, 10), 1: (9, 1, 1)}[b]
        k = len(halos)
        halos.append(
            (
                a,
                b,
                pltpu.make_async_remote_copy(
                    src_ref=E.at[pl.ds(zs[0], zs[1]), pl.ds(xs[0], xs[1])],
                    dst_ref=E.at[pl.ds(zs[2], zs[1]), pl.ds(xs[2], xs[1])],
                    send_sem=send_a.at[k],
                    recv_sem=recv_a.at[k],
                    device_id=(s + a, t + b),
                    device_id_type=MESH,
                ),
            )
        )
    def now(a, b):
        return there(a, b) & jnp.logical_not(opens) if b == -1 else there(a, b)

    def send_halos():
        for a, b, copy in sorted(halos, key=lambda h: -h[1]):

            @pl.when(now(a, b))
            def _():
                copy.start()

    for a in (-1, 0, 1):

        @pl.when(there(a, 1) & closes)
        def _():
            pl.semaphore_signal(cross, inc=1, device_id=(s + a, t + 1), device_id_type=MESH)

    @pl.when(jnp.logical_not(is_source))
    def _():
        send_halos()

    for q in sources:
        sender = sender_of(q)

        @pl.when(late & (sender != t))
        def _():
            pl.semaphore_signal(ready, inc=1, device_id=(s, sender), device_id_type=MESH)

        @pl.when(late & has_outer)
        def _():
            pl.semaphore_signal(ready, inc=1, device_id=(outer, sender), device_id_type=MESH)

    def send(kind, src, d, i):
        own = jnp.int32(i) if isinstance(i, int) else i
        return pltpu.make_async_remote_copy(
            src_ref=src,
            dst_ref=(in_own, in_out)[kind].at[own],
            send_sem=send_b.at[kind],
            recv_sem=recv_b.at[kind, own],
            device_id=((s, outer)[kind], d),
            device_id_type=MESH,
        )

    def to_relay(kind, d, at, z):
        return pltpu.make_async_remote_copy(
            src_ref=(pk_own, pk_out)[kind].at[d],
            dst_ref=(rl_own, rl_out)[kind].at[z],
            send_sem=send_b.at[kind],
            recv_sem=recv_r.at[kind, z],
            device_id=(s, at),
            device_id_type=MESH,
        )

    def to_sibling(i):
        return pltpu.make_async_remote_copy(
            src_ref=in_own.at[i],
            dst_ref=in_sib.at[i],
            send_sem=send_r.at[0],
            recv_sem=recv_b.at[2, i],
            device_id=(sib, t),
            device_id_type=MESH,
        )

    own_slot = t - first

    def relay_columns(z, columns):
        for c in columns:
            d = (col + c) % n_col * NZ + z
            at = (col + c) % n_col * NZ + pos_z
            to_relay(0, d, at, z).start()

            @pl.when(has_outer)
            def _():
                to_relay(1, d, at, z).start()

    def direct_columns(z):
        d = col * NZ + z

        @pl.when(d != t)
        def _():
            send(0, pk_own.at[d], d, own_slot).start()

        @pl.when(has_outer)
        def _():
            send(1, pk_out.at[d], d, own_slot).start()

    @pl.when(is_source)
    def _():
        @pl.loop(0, FIRST)
        def _(z):
            relay_columns(z, (n_col // 2, 1, n_col - 1))
            direct_columns(z)

        send_halos()

        in_own[own_slot] = pk_own[t]

    @pl.when(late)
    def _():
        prepare()

    fine = []
    k0 = len(NEIGHBOURS)
    for a, z in ((1, 7), (-1, 0)):
        slot = 0 if a == 1 else 1
        fine.append((a, 0, rad.at[z], face_rad.at[slot], (s + a, t)))
        fine.append((a, 0, spd.at[z], face_spd.at[slot], (s + a, t)))
    for b in (1, -1):
        slot = 0 if b == 1 else 1
        fine.append((0, b, cols, col_in.at[slot], (s, t + b)))
    fine = [
        (
            a,
            b,
            pltpu.make_async_remote_copy(
                src_ref=src,
                dst_ref=dst,
                send_sem=send_a.at[k0 + i],
                recv_sem=recv_a.at[k0 + i],
                device_id=to,
                device_id_type=MESH,
            ),
        )
        for i, (a, b, src, dst, to) in enumerate(fine)
    ]
    for a, b, copy in fine:

        @pl.when(now(a, b))
        def _():
            copy.start()

    @pl.when(is_source)
    def _():
        @pl.loop(FIRST, EARLY)
        def _(z):
            relay_columns(z, (n_col // 2, 1, n_col - 1))
            direct_columns(z)

        @pl.loop(EARLY, NZ)
        def _(z):
            relay_columns(z, (n_col // 2,))

        @pl.loop(EARLY, NZ)
        def _(z):
            relay_columns(z, (1, n_col - 1))

    def forward(z):
        d = col * NZ + z
        to_relay(0, d, t, z).wait_recv()

        @pl.when(d != t)
        def _():
            send(0, rl_own.at[z], d, relayed).start()

        @pl.when(d == t)
        def _():
            in_own[relayed] = rl_own[z]

        @pl.when(has_outer)
        def _():
            to_relay(1, d, t, z).wait_recv()
            send(1, rl_out.at[z], d, relayed).start()

    @pl.when(is_relay)
    def _():
        @pl.loop(0, EARLY)
        def _(z):
            forward(z)

    @pl.when(late)
    def _():
        prepare_beam()

    def await_halos(before):
        for a, b, copy in halos:
            if (b == 1) == before:

                @pl.when(there(-a, -b))
                def _():
                    copy.wait_recv()

    def edges_of_step():
        @pl.when(s == 0)
        def _():
            M[0:1] = jnp.zeros((1,) + M.shape[1:], F32)

        @pl.when(s == n_slab - 1)
        def _():
            M[5:6] = jnp.zeros((1,) + M.shape[1:], F32)

        @pl.when(t == 0)
        def _():
            M[:, 0:1] = jnp.zeros((6, 1) + M.shape[2:], F32)

        @pl.when(t == n_tile - 1)
        def _():
            M[:, 9:10] = jnp.zeros((6, 1) + M.shape[2:], F32)

    def first_part():
        await_halos(False)
        heat_step(E, PE, M, plane.at[0], depth.at[1:7], 8, 2, 10, 1, slice(2, 12), False)
        edges_of_step()
        heat_step(M, PM, H, plane.at[1], depth.at[2:6], 6, 2, 8, 2, slice(2, 10), False)

    @pl.when(jnp.logical_not(late))
    def _():
        first_part()

    @pl.when(opens & (t > 0))
    def _():
        pl.semaphore_wait(cross, crossing)
        for a, b, copy in halos + fine:
            if b == -1:

                @pl.when(there(a, b))
                def _():
                    copy.start()

    def late_sends():
        @pl.when(sends > 0)
        def _():
            pl.semaphore_wait(ready, n_late)

        @pl.when(is_source)
        def _():
            @pl.loop(EARLY, NZ)
            def _(z):
                direct_columns(z)

        @pl.when(is_relay)
        def _():
            @pl.loop(EARLY, NZ)
            def _(z):
                forward(z)

    late_sends()

    @pl.when(late)
    def _():
        first_part()

    order = (5, 4, 3, 2, 1, 0)
    for i in order:

        @pl.when(sender_of(sources[i]) != t)
        def _():
            send(0, pk_own.at[0], t, i).wait_recv()

        to_sibling(i).start()

    for a, b, copy in fine:

        @pl.when(there(-a, -b))
        def _():
            copy.wait_recv()

    for a, b, copy in fine:

        @pl.when(there(a, b))
        def _():
            copy.wait_send()

    r16 = lax.broadcasted_iota(jnp.int32, (16, 128), 0)
    l16 = lanes(16)
    both = col_in[...].reshape(16, 512)
    tn = (((0,), (0,)), ((), ()))
    s_rad = jnp.where(((r16 == 0) & (l16 == 0)) | ((r16 == 10) & (l16 == 127)), 1.0, 0.0)
    s_spd = jnp.where(((r16 == 1) & (l16 == 0)) | ((r16 == 11) & (l16 == 127)), 1.0, 0.0)
    side_rad[...] = lax.dot_general(
        both, s_rad, tn, precision=hi, preferred_element_type=F32
    ).reshape(8, 64, 128)
    side_spd[...] = lax.dot_general(
        both, s_spd, tn, precision=hi, preferred_element_type=F32
    ).reshape(8, 64, 128)
    for z in range(10):
        Gf[z, 0:8] = jnp.zeros((8, 128), F32)
        Gf[z, 72:80] = jnp.zeros((8, 128), F32)

    await_halos(True)
    heat_step(E, PE, M, plane.at[0], depth.at[1:7], 8, 0, 2, 1, slice(0, 2), True)
    edges_of_step()
    heat_step(M, PM, H, plane.at[1], depth.at[2:6], 6, 0, 2, 2, slice(0, 2), True)

    Hf = H.reshape(4 * 8 * 16, 128)
    for z in range(4):
        for k in range(16):
            heat_out[z, :, 128 * k : 128 * k + 128] = Hf[pl.ds(z * 128 + k, 8, stride=16), :]

    far_lane = jnp.where(lane8 >= 100, lane8 - 125, lane8 - 61)

    def put(i, z, tile, high, halo, base):
        body = pltpu.roll(tile, 64, 1) if high else tile
        around = lane_pick(halo, (far_lane + base) & 127)
        V[z, 8 + 8 * i : 16 + 8 * i] = jnp.where(left, body, around)

    def own_layers(i):
        for z in range(4):
            put(i, 3 + z, in_own[i, z % 2], z >= 2, in_own[i, 2], 6 * z)

    def outer_layers(group):
        @pl.when(has_outer)
        def _():
            for i in group:
                send(1, pk_out.at[0], t, i).wait_recv()
            at = jnp.where(odd, 7, 0)
            base = 64 + jnp.where(odd, 0, 6)
            for i in group:
                for z in range(3):
                    put(i, at + z, in_out[i, z // 2], z == 1, in_out[i, 1], base + 6 * z)

    def sibling_layers(group):
        for i in group:
            to_sibling(i).wait_recv()
        at = jnp.where(odd, 0, 7)
        skip = odd.astype(jnp.int32)
        for i in group:
            halo = in_sib[i, 2]
            for z in range(3):
                tile = in_sib[i, (z + skip) % 2]
                body = jnp.where(z + skip >= 2, pltpu.roll(tile, 64, 1), tile)
                around = lane_pick(halo, (far_lane + 6 * (z + skip)) & 127)
                V[at + z, 8 + 8 * i : 16 + 8 * i] = jnp.where(left, body, around)

    for group in (order,):
        for i in group:
            own_layers(i)
        outer_layers(group)
        sibling_layers(group)

    keep = (lane48 < 64) | ((lane48 < 100) & (t < n_tile - 1)) | ((lane48 >= 100) & (t > 0))
    window_step(V, PV, VM, side[0], depth, 10, keep)

    @pl.when(s == 0)
    def _():
        VM[0:2] = jnp.zeros((2,) + VM.shape[1:], F32)

    @pl.when(s == n_slab - 1)
    def _():
        VM[6:8] = jnp.zeros((2,) + VM.shape[1:], F32)

    window_step(VM, PV.at[0:8], VH, side[1], depth.at[1:7], 8, keep)

    @pl.when(s == 0)
    def _():
        VH[0] = jnp.zeros(VH.shape[1:], F32)

    @pl.when(s == n_slab - 1)
    def _():
        VH[5] = jnp.zeros(VH.shape[1:], F32)

    Xf = X.reshape(6 * 64, 128)
    for z in range(6):
        low, mid, top = VH[z, 15:47], 0.75 * VH[z, 16:48], VH[z, 17:49]
        Xf[pl.ds(64 * z, 32, stride=2), :] = 0.25 * low + mid
        Xf[pl.ds(64 * z + 1, 32, stride=2), :] = mid + 0.25 * top

    lane = lanes(64)
    half = lane >> 1
    near = (half + jnp.where((lane & 1) == 1, 1, -1)) & 127
    fine_y, side_y = [], []
    for z in range(6):
        u = lane_pick(X[z], half)
        v = lane_pick(X[z], near)
        fine_y.append(0.75 * u + 0.25 * v)
        side_y.append(0.75 * v + 0.25 * u)

    def at_height(f, zf):
        z = zf // 2
        if zf % 2 == 0:
            return 0.25 * f[z] + 0.75 * f[z + 1]
        return 0.75 * f[z + 1] + 0.25 * f[z + 2]

    def grow(temp, speed, radius):
        under = jnp.maximum(1.0 - temp, 0.0)
        return radius + speed * under * under

    for zf in range(-1, 9):
        if zf == -1:
            sp, ra = face_spd[0], face_rad[0]
        elif zf == 8:
            sp, ra = face_spd[1], face_rad[1]
        else:
            sp, ra = spd[zf], rad[zf]
        Gf[zf + 1, 8:72] = grow(at_height(fine_y, zf), sp, ra)
    for zf in range(8):
        side = grow(at_height(side_y, zf), side_spd[zf], side_rad[zf])
        c = Gf[zf + 1, 8:72]
        near_y = jnp.maximum(
            jnp.where(lane == 0, side, pltpu.roll(c, 1, 1)),
            jnp.where(lane == 127, side, pltpu.roll(c, 127, 1)),
        )
        near_x = jnp.maximum(Gf[zf + 1, 7:71], Gf[zf + 1, 9:73])
        near_z = jnp.maximum(Gf[zf, 8:72], Gf[zf + 2, 8:72])
        grown_out[zf] = jnp.maximum(c, jnp.maximum(jnp.maximum(near_x, near_y), near_z) - 0.5)
    for a, b, copy in halos:

        @pl.when(there(a, b))
        def _():
            copy.wait_send()

    for i in range(6):
        to_sibling(i).wait_send()

    n_own = jnp.where(is_source, n_tile - 1, 0) + jnp.where(is_relay, NZ - 1, 0)
    n_out = jnp.where(is_source, n_tile, 0) + jnp.where(is_relay, NZ, 0)

    @pl.loop(0, n_own)
    def _(d):
        send(0, pk_own.at[0], t, 0).wait_send()

    @pl.when(has_outer)
    def _():
        @pl.loop(0, n_out)
        def _(d):
            send(1, pk_out.at[0], t, 0).wait_send()


def local(temperature, spot, labels, radius, position, seeds):
    n_slab, n_tile = lax.axis_size("slab"), lax.axis_size("tile")
    any_spec = pl.BlockSpec(memory_space=pl.ANY)
    vm = pltpu.VMEM
    dma = pltpu.SemaphoreType.DMA
    body = lambda *refs: kernel(n_slab, n_tile, *refs)
    return pl.pallas_call(
        body,
        out_shape=(
            vm((4, 8, 2048), F32),
            vm((8, 64, 128), F32),
        ),
        in_specs=[any_spec] * 6,
        out_specs=(pl.BlockSpec(memory_space=pltpu.VMEM),) * 2,
        scratch_shapes=[
            vm((4, 8, 2048), F32),
            pltpu.SMEM((2, 2), jnp.int32),
            vm((8, 64, 128), jnp.int32),
            vm((8, 64, 128), F32),
            vm((64,), jnp.int32),
            vm((64,), jnp.int32),
            vm((8, 64, 128), F32),
            vm((8, 12, 16, 128), F32),
            vm((8, 12, 16, 128), F32),
            vm((6, 10, 16, 128), F32),
            vm((6, 10, 16, 128), F32),
            vm((4, 8, 16, 128), F32),
            vm((2, 12, 16, 128), F32),
            vm((8, 16, 128), F32),
            vm((32, 3, 8, 128), F32),
            vm((32, 2, 8, 128), F32),
            vm((6, 3, 8, 128), F32),
            vm((6, 2, 8, 128), F32),
            vm((6, 3, 8, 128), F32),
            vm((NZ, 3, 8, 128), F32),
            vm((NZ, 2, 8, 128), F32),
            vm((10, 64, 128), F32),
            vm((10, 64, 128), F32),
            vm((8, 64, 128), F32),
            vm((6, 64, 128), F32),
            vm((6, 64, 128), F32),
            vm((2, 64, 128), F32),
            vm((2, 64, 128), F32),
            vm((8, 512), F32),
            vm((2, 8, 512), F32),
            vm((8, 64, 128), F32),
            vm((8, 64, 128), F32),
            vm((10, 80, 128), F32),
            dma((6,)),
            dma((14,)),
            dma((14,)),
            dma((2,)),
            dma((3, 6)),
            dma((2, NZ)),
            dma((1,)),
            pltpu.SemaphoreType.REGULAR,
            pltpu.SemaphoreType.REGULAR,
            vm((2, 48, 128), F32),
        ],
        compiler_params=pltpu.CompilerParams(collective_id=0, has_side_effects=True),
        name="build_step",
    )(temperature, spot, labels, radius, position, seeds)


def solution(mesh):
    return jax.shard_map(
        local,
        mesh=mesh,
        in_specs=(
            P("slab", "tile", None),
            P(),
            P("slab", None, "tile"),
            P("slab", None, "tile"),
            P(("slab", "tile")),
            P(("slab", "tile")),
        ),
        out_specs=(P("slab", "tile", None), P("slab", None, "tile")),
        check_vma=False,
    )
```

```python
import jax
import jax.numpy as jnp
from jax import lax
from jax.experimental import pallas as pl
from jax.experimental.pallas import tpu as pltpu
from jax.sharding import PartitionSpec as P

HEAT_RATE = 0.1
SOURCE_POWER = 1.5
BEAM_RADIUS_SQ = 36.0
DEPTH_SCALE = 3.0
GOLDEN_ANGLE = 2.39996323
MESH = pl.DeviceIdType.MESH
NZ = 8
FIRST, EARLY = 2, 4
F32 = jnp.float32
NEIGHBOURS = [(a, b) for a in (-1, 0, 1) for b in (-1, 0, 1) if (a, b) != (0, 0)]


def lanes(rows):
    return lax.broadcasted_iota(jnp.int32, (rows, 128), 1)


def lane_pick(x, index):
    return jnp.take_along_axis(x, index, axis=1)


def conductance(v):
    return 0.5 * HEAT_RATE * 1.5 - (0.25 * HEAT_RATE) / (1.0 + v * v)


def next_along_y(x, last):
    r = pltpu.roll(x, 127, 2)
    up = pltpu.roll(r, 15, 1)
    lane = lax.broadcasted_iota(jnp.int32, x.shape, 2)
    row = lax.broadcasted_iota(jnp.int32, x.shape, 1)
    up = jnp.where(row == 15, last, up)
    return jnp.where(lane == 127, up, r)


def before_along_y(x, first):
    r = pltpu.roll(x, 1, 2)
    down = pltpu.roll(r, 1, 1)
    lane = lax.broadcasted_iota(jnp.int32, x.shape, 2)
    row = lax.broadcasted_iota(jnp.int32, x.shape, 1)
    down = jnp.where(row == 0, first, down)
    return jnp.where(lane == 0, down, r)


def heat_step(src, cond, dst, plane, depth, count_z, first_x, last_x, offset_x, fill, unroll):
    wide, inner = slice(first_x, last_x + 2), slice(first_x + 1, last_x + 1)

    def conductances(z, c):
        cond[z, fill] = conductance(src[z, fill])
        return c

    lax.fori_loop(0, count_z, conductances, 0, unroll=unroll)

    def layer(z, c):
        v = src[z + 1, wide]
        p = cond[z + 1, wide]
        flux_x = (p[:-1] + p[1:]) * (v[1:] - v[:-1])
        vc, pc = v[1:-1], p[1:-1]
        total = flux_x[1:] - flux_x[:-1]
        total += (pc + cond[z, inner]) * (src[z, inner] - vc)
        total += (pc + cond[z + 2, inner]) * (src[z + 2, inner] - vc)
        outside = 0.5 * HEAT_RATE
        flux_y = (pc + next_along_y(pc, outside)) * (next_along_y(vc, 0.0) - vc)
        edge = (pc + outside) * vc
        low = jnp.broadcast_to(edge[:, 0:1, 0:1], vc.shape)
        total += flux_y - before_along_y(flux_y, low)
        source = plane[offset_x + first_x : offset_x + last_x] * depth[z]
        dst[z, first_x:last_x] = vc + total + source
        return c

    lax.fori_loop(0, count_z - 2, layer, 0, unroll=unroll)


def window_step(src, cond, dst, plane, depth, count_z, keep):
    for z in range(count_z):
        cond[z] = conductance(src[z])
    for z in range(count_z - 2):
        v, p = src[z + 1, 8:56], cond[z + 1, 8:56]
        total = (p + cond[z, 8:56]) * (src[z, 8:56] - v)
        total += (p + cond[z + 2, 8:56]) * (src[z + 2, 8:56] - v)
        total += (p + cond[z + 1, 7:55]) * (src[z + 1, 7:55] - v)
        total += (p + cond[z + 1, 9:57]) * (src[z + 1, 9:57] - v)
        total += (p + pltpu.roll(p, 1, 1)) * (pltpu.roll(v, 1, 1) - v)
        total += (p + pltpu.roll(p, 127, 1)) * (pltpu.roll(v, 127, 1) - v)
        at = jnp.broadcast_to(depth[z, 0:1, :], v.shape)
        dst[z, 8:56] = jnp.where(keep, v + total + plane * at, 0.0)


def kernel(
    n_slab,
    n_tile,
    x_in,
    spot_in,
    lab_in,
    rad_in,
    pos_in,
    seed_in,
    heat_out,
    grown_out,
    x_v,
    spot,
    lab,
    rad,
    pos,
    seed,
    spd,
    E,
    PE,
    M,
    PM,
    H,
    plane,
    depth,
    pk_own,
    pk_out,
    in_own,
    in_out,
    in_sib,
    rl_own,
    rl_out,
    V,
    PV,
    VM,
    VH,
    X,
    face_rad,
    face_spd,
    cols,
    col_in,
    side_rad,
    side_spd,
    Gf,
    in_sem,
    send_a,
    recv_a,
    send_b,
    recv_b,
    recv_r,
    send_r,
    ready,
    cross,
    side,
):
    s = lax.axis_index("slab")
    t = lax.axis_index("tile")
    first = n_tile // 2 - 3
    sources = tuple(range(first, first + 6))
    is_source = (t >= first) & (t < first + 6)
    n_col = n_tile // NZ
    col, pos_z = t // NZ, t % NZ
    odd = s % 2 == 1
    sib = jnp.where(odd, s - 1, s + 1)
    outer = jnp.where(odd, s + 1, s - 1)
    has_outer = (outer >= 0) & (outer < n_slab)

    def sender_of(q):
        return col * NZ + q % NZ

    relayed = jnp.int32(0)
    is_relay = jnp.bool_(False)
    for i, q in enumerate(sources):
        mine = (pos_z == q % NZ) & ((col != q // NZ))
        relayed = jnp.where(mine, i, relayed)
        is_relay = is_relay | mine

    def there(a, b):
        c = jnp.bool_(True)
        if a == -1:
            c = c & (s > 0)
        if a == 1:
            c = c & (s < n_slab - 1)
        if b == -1:
            c = c & (t > 0)
        if b == 1:
            c = c & (t < n_tile - 1)
        return c

    bar = pltpu.get_barrier_semaphore()

    @pl.when(is_relay)
    def _():
        pl.semaphore_signal(bar, inc=1, device_id=(s, first + relayed), device_id_type=MESH)

    outer_one = has_outer.astype(jnp.int32)

    @pl.when(is_source | is_relay)
    def _():
        for z in range(EARLY, NZ):
            d = col * NZ + z
            apart = jnp.abs(pos_z - z) > 1

            @pl.when(apart)
            def _():
                pl.semaphore_signal(bar, inc=1, device_id=(s, d), device_id_type=MESH)

            @pl.when(apart & has_outer)
            def _():
                pl.semaphore_signal(bar, inc=1, device_id=(outer, d), device_id_type=MESH)

    loads = [
        pltpu.make_async_copy(a, b, in_sem.at[i])
        for i, (a, b) in enumerate(
            (
                (x_in, x_v),
                (lab_in, lab),
                (rad_in, rad),
                (spot_in, spot),
                (pos_in, pos),
                (seed_in, seed),
            )
        )
    ]
    for c in loads:
        c.start()

    late = pos_z >= EARLY
    opens, closes = pos_z == 0, pos_z == NZ - 1
    count = jnp.int32(0)
    crossing = jnp.int32(0)
    for a, b in NEIGHBOURS:
        c = there(a, b)
        later = c & closes if b == 1 else jnp.bool_(False)
        across = c & opens if b == -1 else jnp.bool_(False)

        @pl.when(c & jnp.logical_not(later))
        def _():
            pl.semaphore_signal(bar, inc=1, device_id=(s + a, t + b), device_id_type=MESH)

        count = count + (c & jnp.logical_not(across)).astype(jnp.int32)
        crossing = crossing + across.astype(jnp.int32)
    for q in sources:
        sender = sender_of(q)

        @pl.when((sender != t) & jnp.logical_not(late))
        def _():
            pl.semaphore_signal(bar, inc=1, device_id=(s, sender), device_id_type=MESH)

        @pl.when(has_outer & jnp.logical_not(late))
        def _():
            pl.semaphore_signal(bar, inc=1, device_id=(outer, sender), device_id_type=MESH)

        apart = jnp.abs(pos_z - q % NZ) > 1
        count = count + jnp.where(late & apart, 1 + outer_one, 0)

    sends = jnp.where(is_source | is_relay, 1, 0)
    me_late = late.astype(jnp.int32)
    n_early = sends * EARLY * (1 + outer_one) - sends * (1 - me_late)
    n_late = sends * (NZ - EARLY) * (1 + outer_one) - sends * me_late
    count = count + n_early + jnp.where(is_source, n_col - 1, 0)

    @pl.when(s == 0)
    def _():
        E[0:2] = jnp.zeros((2,) + E.shape[1:], F32)
        V[0:3] = jnp.zeros((3,) + V.shape[1:], F32)
        face_rad[0] = jnp.zeros((64, 128), F32)
        face_spd[0] = jnp.zeros((64, 128), F32)

    @pl.when(s == n_slab - 1)
    def _():
        E[6:8] = jnp.zeros((2,) + E.shape[1:], F32)
        V[7:10] = jnp.zeros((3,) + V.shape[1:], F32)
        face_rad[1] = jnp.zeros((64, 128), F32)
        face_spd[1] = jnp.zeros((64, 128), F32)

    @pl.when(t == 0)
    def _():
        E[:, 0:2] = jnp.zeros((8, 2) + E.shape[2:], F32)
        col_in[0] = jnp.zeros(col_in.shape[1:], F32)

    @pl.when(t == n_tile - 1)
    def _():
        E[:, 10:12] = jnp.zeros((8, 2) + E.shape[2:], F32)
        col_in[1] = jnp.zeros(col_in.shape[1:], F32)

    loads[0].wait()
    flat = E.reshape(8 * 12 * 16, 128)
    for z in range(4):
        for k in range(16):
            row = ((z + 2) * 12 + 2) * 16 + k
            flat[pl.ds(row, 8, stride=16), :] = x_v[z, :, 128 * k : 128 * k + 128]

    lane8 = lanes(8)
    left = lane8 < 64

    @pl.when(is_source)
    def _():
        def read(z, k):
            if k < 0 or k > 15:
                return jnp.zeros((8, 128), F32)
            return x_v[z, :, 128 * k : 128 * k + 128]

        for k in range(16):
            now = [read(z, k) for z in range(4)]
            turned = [pltpu.roll(v, 64, 1) for v in now]
            h_even = jnp.zeros((8, 128), F32)
            h_odd = jnp.zeros((8, 128), F32)
            for z in range(4):
                low, top = read(z, k - 1), read(z, k + 1)
                here = pltpu.roll(now[z], 67 + 6 * z, 1)
                low = pltpu.roll(low, 3 + 6 * z, 1)
                top = pltpu.roll(top, 3 + 6 * z, 1)
                one = (lane8 >= 6 * z) & (lane8 < 6 * z + 3)
                two = (lane8 >= 6 * z + 3) & (lane8 < 6 * z + 6)
                h_even = jnp.where(one, low, jnp.where(two, here, h_even))
                h_odd = jnp.where(one, here, jnp.where(two, top, h_odd))
            for parity, lo, up, halo in ((0, now, turned, h_even), (1, turned, now, h_odd)):
                d = 2 * k + parity
                far = pltpu.roll(halo, 64, 1)
                pk_own[d, 0] = jnp.where(left, lo[0], up[2])
                pk_own[d, 1] = jnp.where(left, lo[1], up[3])
                pk_own[d, 2] = halo
                pk_out[d, 0] = jnp.where(
                    left, jnp.where(odd, lo[1], lo[0]), jnp.where(odd, up[2], up[1])
                )
                pk_out[d, 1] = jnp.where(left, jnp.where(odd, lo[3], lo[2]), far)

    hi = lax.Precision.HIGHEST
    pick_r = lax.broadcasted_iota(jnp.int32, (8, 128), 0)
    lane48 = lanes(48)
    wy = t * 64 + lane48 - jnp.where(lane48 < 100, 0, 128)
    wx = lax.broadcasted_iota(jnp.int32, (48, 128), 0) + first * 8
    def prepare():
        for c in loads[1:]:
            c.wait()
        place = pos[...].reshape(1, 64)
        value = ((seed[...].reshape(1, 64) & 63) + 1).astype(F32)
        rows = lax.broadcasted_iota(jnp.int32, (512, 64), 0)
        cells = lax.broadcasted_iota(jnp.int32, (128, 64), 0)
        in_row = jnp.where(rows == (place >> 7), 1.0, 0.0).astype(jnp.bfloat16)
        in_lane = jnp.where(cells == (place & 127), value, 0.0).astype(jnp.bfloat16)
        named = lax.dot_general(
            in_row, in_lane, (((1,), (1,)), ((), ())), preferred_element_type=F32
        ).reshape(8, 64, 128)
        theta = GOLDEN_ANGLE * lanes(8).astype(F32)
        table = 1.0 + 0.5 * jnp.cos(4.0 * theta)
        table = jnp.broadcast_to(table[0:1], (64, 128))
        for z in range(8):
            grain = jnp.where(named[z] > 0.5, named[z].astype(jnp.int32) - 1, lab[z] & 63)
            spd[z] = lane_pick(table, grain)

        nt = (((1,), (1,)), ((), ()))
        e_rad = jnp.where(
            ((pick_r == 0) & (lane8 == 127)) | ((pick_r == 2) & (lane8 == 0)), 1.0, 0.0
        )
        e_spd = jnp.where(
            ((pick_r == 1) & (lane8 == 127)) | ((pick_r == 3) & (lane8 == 0)), 1.0, 0.0
        )
        cols[...] = lax.dot_general(
            e_rad, rad[...].reshape(512, 128), nt, precision=hi, preferred_element_type=F32
        ) + lax.dot_general(
            e_spd, spd[...].reshape(512, 128), nt, precision=hi, preferred_element_type=F32
        )

    def prepare_beam():
        for step in range(2):
            row = lax.broadcasted_iota(jnp.int32, (12, 16, 128), 0)
            y = lax.broadcasted_iota(jnp.int32, (12, 16, 128), 1) * 128
            y = y + lax.broadcasted_iota(jnp.int32, (12, 16, 128), 2)
            xd = (t * 8 - 2 + row - spot[step, 0]).astype(F32)
            yd = (y - spot[step, 1]).astype(F32)
            plane[step] = SOURCE_POWER * jnp.exp(-(xd * xd + yd * yd) / BEAM_RADIUS_SQ)
            xd = (wx - spot[step, 0]).astype(F32)
            yd = (wy - spot[step, 1]).astype(F32)
            side[step] = SOURCE_POWER * jnp.exp(-(xd * xd + yd * yd) / BEAM_RADIUS_SQ)
        level = lax.broadcasted_iota(jnp.int32, (8, 16, 128), 0) + (s * 4 - 2)
        depth[...] = jnp.exp(-(n_slab * 4 - 1 - level).astype(F32) / DEPTH_SCALE)


    @pl.when(jnp.logical_not(late))
    def _():
        prepare()
        prepare_beam()

    pl.semaphore_wait(bar, count)

    halos = []
    for a, b in NEIGHBOURS:
        zs = {0: (2, 4, 2), -1: (2, 2, 6), 1: (4, 2, 0)}[a]
        xs = {0: (2, 8, 2), -1: (2, 2, 10), 1: (8, 2, 0)}[b]
        if a != 0 and b != 0:
            zs = {-1: (2, 1, 6), 1: (5, 1, 1)}[a]
            xs = {-1: (2, 1, 10), 1: (9, 1, 1)}[b]
        k = len(halos)
        halos.append(
            (
                a,
                b,
                pltpu.make_async_remote_copy(
                    src_ref=E.at[pl.ds(zs[0], zs[1]), pl.ds(xs[0], xs[1])],
                    dst_ref=E.at[pl.ds(zs[2], zs[1]), pl.ds(xs[2], xs[1])],
                    send_sem=send_a.at[k],
                    recv_sem=recv_a.at[k],
                    device_id=(s + a, t + b),
                    device_id_type=MESH,
                ),
            )
        )
    def now(a, b):
        return there(a, b) & jnp.logical_not(opens) if b == -1 else there(a, b)

    def send_halos():
        for a, b, copy in sorted(halos, key=lambda h: (-h[1], abs(h[0]))):

            @pl.when(now(a, b))
            def _():
                copy.start()

    for a in (-1, 0, 1):

        @pl.when(there(a, 1) & closes)
        def _():
            pl.semaphore_signal(cross, inc=1, device_id=(s + a, t + 1), device_id_type=MESH)

    @pl.when(jnp.logical_not(is_source))
    def _():
        send_halos()

    for q in sources:
        sender = sender_of(q)

        @pl.when(late & (sender != t))
        def _():
            pl.semaphore_signal(ready, inc=1, device_id=(s, sender), device_id_type=MESH)

        @pl.when(late & has_outer)
        def _():
            pl.semaphore_signal(ready, inc=1, device_id=(outer, sender), device_id_type=MESH)

    def send(kind, src, d, i):
        own = jnp.int32(i) if isinstance(i, int) else i
        return pltpu.make_async_remote_copy(
            src_ref=src,
            dst_ref=(in_own, in_out)[kind].at[own],
            send_sem=send_b.at[kind],
            recv_sem=recv_b.at[kind, own],
            device_id=((s, outer)[kind], d),
            device_id_type=MESH,
        )

    def to_relay(kind, d, at, z):
        return pltpu.make_async_remote_copy(
            src_ref=(pk_own, pk_out)[kind].at[d],
            dst_ref=(rl_own, rl_out)[kind].at[z],
            send_sem=send_b.at[kind],
            recv_sem=recv_r.at[kind, z],
            device_id=(s, at),
            device_id_type=MESH,
        )

    def to_sibling(i):
        return pltpu.make_async_remote_copy(
            src_ref=in_own.at[i],
            dst_ref=in_sib.at[i],
            send_sem=send_r.at[0],
            recv_sem=recv_b.at[2, i],
            device_id=(sib, t),
            device_id_type=MESH,
        )

    own_slot = t - first

    def relay_columns(z, columns):
        for c in columns:
            d = (col + c) % n_col * NZ + z
            at = (col + c) % n_col * NZ + pos_z
            to_relay(0, d, at, z).start()

            @pl.when(has_outer)
            def _():
                to_relay(1, d, at, z).start()

    def direct_columns(z):
        d = col * NZ + z

        @pl.when(d != t)
        def _():
            send(0, pk_own.at[d], d, own_slot).start()

        @pl.when(has_outer)
        def _():
            send(1, pk_out.at[d], d, own_slot).start()

    @pl.when(is_source)
    def _():
        @pl.loop(0, FIRST)
        def _(z):
            relay_columns(z, (n_col // 2, 1, n_col - 1))
            direct_columns(z)

        send_halos()

        in_own[own_slot] = pk_own[t]

    @pl.when(late)
    def _():
        prepare()

    fine = []
    k0 = len(NEIGHBOURS)
    for a, z in ((1, 7), (-1, 0)):
        slot = 0 if a == 1 else 1
        fine.append((a, 0, rad.at[z], face_rad.at[slot], (s + a, t)))
        fine.append((a, 0, spd.at[z], face_spd.at[slot], (s + a, t)))
    for b in (1, -1):
        slot = 0 if b == 1 else 1
        fine.append((0, b, cols, col_in.at[slot], (s, t + b)))
    fine = [
        (
            a,
            b,
            pltpu.make_async_remote_copy(
                src_ref=src,
                dst_ref=dst,
                send_sem=send_a.at[k0 + i],
                recv_sem=recv_a.at[k0 + i],
                device_id=to,
                device_id_type=MESH,
            ),
        )
        for i, (a, b, src, dst, to) in enumerate(fine)
    ]
    for a, b, copy in fine:

        @pl.when(now(a, b))
        def _():
            copy.start()

    @pl.when(is_source)
    def _():
        @pl.loop(FIRST, EARLY)
        def _(z):
            relay_columns(z, (n_col // 2, 1, n_col - 1))
            direct_columns(z)

        @pl.loop(EARLY, NZ)
        def _(z):
            relay_columns(z, (n_col // 2,))

        @pl.loop(EARLY, NZ)
        def _(z):
            relay_columns(z, (1, n_col - 1))

    def forward(z):
        d = col * NZ + z
        to_relay(0, d, t, z).wait_recv()

        @pl.when(d != t)
        def _():
            send(0, rl_own.at[z], d, relayed).start()

        @pl.when(d == t)
        def _():
            in_own[relayed] = rl_own[z]

        @pl.when(has_outer)
        def _():
            to_relay(1, d, t, z).wait_recv()
            send(1, rl_out.at[z], d, relayed).start()

    @pl.when(is_relay)
    def _():
        @pl.loop(0, EARLY)
        def _(z):
            forward(z)

    @pl.when(late)
    def _():
        prepare_beam()

    def await_halos(before):
        for a, b, copy in halos:
            if (b == 1) == before:

                @pl.when(there(-a, -b))
                def _():
                    copy.wait_recv()

    def edges_of_step():
        @pl.when(s == 0)
        def _():
            M[0:1] = jnp.zeros((1,) + M.shape[1:], F32)

        @pl.when(s == n_slab - 1)
        def _():
            M[5:6] = jnp.zeros((1,) + M.shape[1:], F32)

        @pl.when(t == 0)
        def _():
            M[:, 0:1] = jnp.zeros((6, 1) + M.shape[2:], F32)

        @pl.when(t == n_tile - 1)
        def _():
            M[:, 9:10] = jnp.zeros((6, 1) + M.shape[2:], F32)

    def first_part():
        await_halos(False)
        heat_step(E, PE, M, plane.at[0], depth.at[1:7], 8, 2, 10, 1, slice(2, 12), False)
        edges_of_step()
        heat_step(M, PM, H, plane.at[1], depth.at[2:6], 6, 2, 8, 2, slice(2, 10), False)

    @pl.when(jnp.logical_not(late))
    def _():
        first_part()

    @pl.when(opens & (t > 0))
    def _():
        pl.semaphore_wait(cross, crossing)
        for a, b, copy in halos + fine:
            if b == -1:

                @pl.when(there(a, b))
                def _():
                    copy.start()

    def late_sends():
        @pl.when(sends > 0)
        def _():
            pl.semaphore_wait(ready, n_late)

        @pl.when(is_source)
        def _():
            @pl.loop(EARLY, NZ)
            def _(z):
                direct_columns(z)

        @pl.when(is_relay)
        def _():
            @pl.loop(EARLY, NZ)
            def _(z):
                forward(z)

    late_sends()

    @pl.when(late)
    def _():
        first_part()

    order = (5, 4, 3, 2, 1, 0)
    for i in order:

        @pl.when(sender_of(sources[i]) != t)
        def _():
            send(0, pk_own.at[0], t, i).wait_recv()

        to_sibling(i).start()

    for a, b, copy in fine:

        @pl.when(there(-a, -b))
        def _():
            copy.wait_recv()

    for a, b, copy in fine:

        @pl.when(there(a, b))
        def _():
            copy.wait_send()

    r16 = lax.broadcasted_iota(jnp.int32, (16, 128), 0)
    l16 = lanes(16)
    both = col_in[...].reshape(16, 512)
    tn = (((0,), (0,)), ((), ()))
    s_rad = jnp.where(((r16 == 0) & (l16 == 0)) | ((r16 == 10) & (l16 == 127)), 1.0, 0.0)
    s_spd = jnp.where(((r16 == 1) & (l16 == 0)) | ((r16 == 11) & (l16 == 127)), 1.0, 0.0)
    side_rad[...] = lax.dot_general(
        both, s_rad, tn, precision=hi, preferred_element_type=F32
    ).reshape(8, 64, 128)
    side_spd[...] = lax.dot_general(
        both, s_spd, tn, precision=hi, preferred_element_type=F32
    ).reshape(8, 64, 128)
    for z in range(10):
        Gf[z, 0:8] = jnp.zeros((8, 128), F32)
        Gf[z, 72:80] = jnp.zeros((8, 128), F32)

    await_halos(True)
    heat_step(E, PE, M, plane.at[0], depth.at[1:7], 8, 0, 2, 1, slice(0, 2), True)
    edges_of_step()
    heat_step(M, PM, H, plane.at[1], depth.at[2:6], 6, 0, 2, 2, slice(0, 2), True)

    Hf = H.reshape(4 * 8 * 16, 128)
    for z in range(4):
        for k in range(16):
            heat_out[z, :, 128 * k : 128 * k + 128] = Hf[pl.ds(z * 128 + k, 8, stride=16), :]

    far_lane = jnp.where(lane8 >= 100, lane8 - 125, lane8 - 61)

    def put(i, z, tile, high, halo, base):
        body = pltpu.roll(tile, 64, 1) if high else tile
        around = lane_pick(halo, (far_lane + base) & 127)
        V[z, 8 + 8 * i : 16 + 8 * i] = jnp.where(left, body, around)

    def own_layers(i):
        for z in range(4):
            put(i, 3 + z, in_own[i, z % 2], z >= 2, in_own[i, 2], 6 * z)

    def outer_layers(group):
        @pl.when(has_outer)
        def _():
            for i in group:
                send(1, pk_out.at[0], t, i).wait_recv()
            at = jnp.where(odd, 7, 0)
            base = 64 + jnp.where(odd, 0, 6)
            for i in group:
                for z in range(3):
                    put(i, at + z, in_out[i, z // 2], z == 1, in_out[i, 1], base + 6 * z)

    def sibling_layers(group):
        for i in group:
            to_sibling(i).wait_recv()
        at = jnp.where(odd, 0, 7)
        skip = odd.astype(jnp.int32)
        for i in group:
            halo = in_sib[i, 2]
            for z in range(3):
                tile = in_sib[i, (z + skip) % 2]
                body = jnp.where(z + skip >= 2, pltpu.roll(tile, 64, 1), tile)
                around = lane_pick(halo, (far_lane + 6 * (z + skip)) & 127)
                V[at + z, 8 + 8 * i : 16 + 8 * i] = jnp.where(left, body, around)

    for group in (order,):
        for i in group:
            own_layers(i)
        outer_layers(group)
        sibling_layers(group)

    keep = (lane48 < 64) | ((lane48 < 100) & (t < n_tile - 1)) | ((lane48 >= 100) & (t > 0))
    window_step(V, PV, VM, side[0], depth, 10, keep)

    @pl.when(s == 0)
    def _():
        VM[0:2] = jnp.zeros((2,) + VM.shape[1:], F32)

    @pl.when(s == n_slab - 1)
    def _():
        VM[6:8] = jnp.zeros((2,) + VM.shape[1:], F32)

    window_step(VM, PV.at[0:8], VH, side[1], depth.at[1:7], 8, keep)

    @pl.when(s == 0)
    def _():
        VH[0] = jnp.zeros(VH.shape[1:], F32)

    @pl.when(s == n_slab - 1)
    def _():
        VH[5] = jnp.zeros(VH.shape[1:], F32)

    Xf = X.reshape(6 * 64, 128)
    for z in range(6):
        low, mid, top = VH[z, 15:47], 0.75 * VH[z, 16:48], VH[z, 17:49]
        Xf[pl.ds(64 * z, 32, stride=2), :] = 0.25 * low + mid
        Xf[pl.ds(64 * z + 1, 32, stride=2), :] = mid + 0.25 * top

    lane = lanes(64)
    half = lane >> 1
    near = (half + jnp.where((lane & 1) == 1, 1, -1)) & 127
    fine_y, side_y = [], []
    for z in range(6):
        u = lane_pick(X[z], half)
        v = lane_pick(X[z], near)
        fine_y.append(0.75 * u + 0.25 * v)
        side_y.append(0.75 * v + 0.25 * u)

    def at_height(f, zf):
        z = zf // 2
        if zf % 2 == 0:
            return 0.25 * f[z] + 0.75 * f[z + 1]
        return 0.75 * f[z + 1] + 0.25 * f[z + 2]

    def grow(temp, speed, radius):
        under = jnp.maximum(1.0 - temp, 0.0)
        return radius + speed * under * under

    for zf in range(-1, 9):
        if zf == -1:
            sp, ra = face_spd[0], face_rad[0]
        elif zf == 8:
            sp, ra = face_spd[1], face_rad[1]
        else:
            sp, ra = spd[zf], rad[zf]
        Gf[zf + 1, 8:72] = grow(at_height(fine_y, zf), sp, ra)
    for zf in range(8):
        side = grow(at_height(side_y, zf), side_spd[zf], side_rad[zf])
        c = Gf[zf + 1, 8:72]
        near_y = jnp.maximum(
            jnp.where(lane == 0, side, pltpu.roll(c, 1, 1)),
            jnp.where(lane == 127, side, pltpu.roll(c, 127, 1)),
        )
        near_x = jnp.maximum(Gf[zf + 1, 7:71], Gf[zf + 1, 9:73])
        near_z = jnp.maximum(Gf[zf, 8:72], Gf[zf + 2, 8:72])
        grown_out[zf] = jnp.maximum(c, jnp.maximum(jnp.maximum(near_x, near_y), near_z) - 0.5)
    for a, b, copy in halos:

        @pl.when(there(a, b))
        def _():
            copy.wait_send()

    for i in range(6):
        to_sibling(i).wait_send()

    n_own = jnp.where(is_source, n_tile - 1, 0) + jnp.where(is_relay, NZ - 1, 0)
    n_out = jnp.where(is_source, n_tile, 0) + jnp.where(is_relay, NZ, 0)

    @pl.loop(0, n_own)
    def _(d):
        send(0, pk_own.at[0], t, 0).wait_send()

    @pl.when(has_outer)
    def _():
        @pl.loop(0, n_out)
        def _(d):
            send(1, pk_out.at[0], t, 0).wait_send()


def local(temperature, spot, labels, radius, position, seeds):
    n_slab, n_tile = lax.axis_size("slab"), lax.axis_size("tile")
    any_spec = pl.BlockSpec(memory_space=pl.ANY)
    vm = pltpu.VMEM
    dma = pltpu.SemaphoreType.DMA
    body = lambda *refs: kernel(n_slab, n_tile, *refs)
    return pl.pallas_call(
        body,
        out_shape=(
            vm((4, 8, 2048), F32),
            vm((8, 64, 128), F32),
        ),
        in_specs=[any_spec] * 6,
        out_specs=(pl.BlockSpec(memory_space=pltpu.VMEM),) * 2,
        scratch_shapes=[
            vm((4, 8, 2048), F32),
            pltpu.SMEM((2, 2), jnp.int32),
            vm((8, 64, 128), jnp.int32),
            vm((8, 64, 128), F32),
            vm((64,), jnp.int32),
            vm((64,), jnp.int32),
            vm((8, 64, 128), F32),
            vm((8, 12, 16, 128), F32),
            vm((8, 12, 16, 128), F32),
            vm((6, 10, 16, 128), F32),
            vm((6, 10, 16, 128), F32),
            vm((4, 8, 16, 128), F32),
            vm((2, 12, 16, 128), F32),
            vm((8, 16, 128), F32),
            vm((32, 3, 8, 128), F32),
            vm((32, 2, 8, 128), F32),
            vm((6, 3, 8, 128), F32),
            vm((6, 2, 8, 128), F32),
            vm((6, 3, 8, 128), F32),
            vm((NZ, 3, 8, 128), F32),
            vm((NZ, 2, 8, 128), F32),
            vm((10, 64, 128), F32),
            vm((10, 64, 128), F32),
            vm((8, 64, 128), F32),
            vm((6, 64, 128), F32),
            vm((6, 64, 128), F32),
            vm((2, 64, 128), F32),
            vm((2, 64, 128), F32),
            vm((8, 512), F32),
            vm((2, 8, 512), F32),
            vm((8, 64, 128), F32),
            vm((8, 64, 128), F32),
            vm((10, 80, 128), F32),
            dma((6,)),
            dma((14,)),
            dma((14,)),
            dma((2,)),
            dma((3, 6)),
            dma((2, NZ)),
            dma((1,)),
            pltpu.SemaphoreType.REGULAR,
            pltpu.SemaphoreType.REGULAR,
            vm((2, 48, 128), F32),
        ],
        compiler_params=pltpu.CompilerParams(collective_id=0, has_side_effects=True),
        name="build_step",
    )(temperature, spot, labels, radius, position, seeds)


def solution(mesh):
    return jax.shard_map(
        local,
        mesh=mesh,
        in_specs=(
            P("slab", "tile", None),
            P(),
            P("slab", None, "tile"),
            P("slab", None, "tile"),
            P(("slab", "tile")),
            P(("slab", "tile")),
        ),
        out_specs=(P("slab", "tile", None), P("slab", None, "tile")),
        check_vma=False,
    )
```
